32 devices in a mesh: expert: 4 (over z), fsdp: 8 (over y, x, core).
Axes of the slice: x: 2, y: 2, z: 4, core: 2. Of those that a mesh axis runs over, the one named last changes fastest.
Arguments:
- tokens: bfloat16 [8192, 2048], P(('expert', 'fsdp')), may hold values from -6 to 6
- expert_ids: int32 [8192, 6], P(('expert', 'fsdp')), may hold values from 0 to 63, as said below
- gate_vals: bfloat16 [8192, 6], P(('expert', 'fsdp')), may hold values from 0.099609375 to 1
- w_gate: bfloat16 [4, 2048, 1408], P('expert', 'fsdp'), may hold values from -0.125 to 0.125
- w_up: bfloat16 [4, 2048, 1408], P('expert', 'fsdp'), may hold values from -0.125 to 0.125
- w_down: bfloat16 [4, 2048, 1408], P('expert', 'fsdp'), may hold values from -0.15625 to 0.15625
- cotangent: bfloat16 [8192, 2048], P(('expert', 'fsdp')), may hold values from -6 to 6
Outputs:
- output: bfloat16 [8192, 2048], P(('expert', 'fsdp'))
- grad_tokens: bfloat16 [8192, 2048], P(('expert', 'fsdp'))
- grad_gates: float32 [8192, 6], P(('expert', 'fsdp'))
- grad_w_gate: float32 [4, 2048, 1408], P('expert', 'fsdp')
- grad_w_up: float32 [4, 2048, 1408], P('expert', 'fsdp')
- grad_w_down: float32 [4, 2048, 1408], P('expert', 'fsdp')
The draws below stay inside these ranges and needn't reach their ends.
Inputs may be any that keep to these rules, and one draw needn't show every extreme that they name: `expert_ids`: each row names 6 different experts. Among the tokens of one device at most 48 name any one expert whose number modulo 16 is below 1. On every device some such expert is named by exactly 48 of its tokens, and for every column one such expert is named by exactly 48 tokens of every device of that column.
All inputs are finite; a program needn't handle non-finite values.
Results may differ from the reference program's by a relative error of at most 0.013.
Values may be sent and summed in bfloat16 or wider, within the bound.
A program may use at most 128 MiB of HBM per device.

```python
import jax
import jax.numpy as jnp
from jax import lax

D = 2048
FF = 1408
EXPERTS = 64
TOP = 6
TOK_DEV = 256
WAVE = 1
GROUPS = 4
COLUMNS = 8
PER_INDEX = 16
WINDOW = 4
MOST = 48
TOKENS = 8192


def block_routes(key, block):
    column_index = block % COLUMNS
    hot_pick = jax.random.randint(jax.random.fold_in(key, 7), (COLUMNS,), 0, WINDOW)[column_index]
    block_key = jax.random.fold_in(key, block + 11)
    key_shift, key_perm, key_score, key_order = jax.random.split(block_key, 4)
    shifts = jax.random.randint(key_shift, (WINDOW,), 0, 3)
    levels = jnp.array([MOST, MOST // 2, MOST // 4], jnp.int32)
    counts = levels[shifts]
    counts = jnp.where(jnp.arange(WINDOW) == hot_pick, MOST, counts).astype(jnp.int32)
    starts = jnp.cumsum(counts) - counts
    position = jnp.arange(TOK_DEV, dtype=jnp.int32)
    covered = (position[:, None] - starts[None, :]) % TOK_DEV < counts[None, :]
    shuffle = jax.random.permutation(key_perm, TOK_DEV)
    token_cover = covered[shuffle]
    window_ids = jnp.arange(WINDOW, dtype=jnp.int32)
    window_expert = window_ids // WAVE * PER_INDEX + window_ids % WAVE
    cover_full = jnp.zeros((TOK_DEV, EXPERTS), jnp.bool_).at[:, window_expert].set(token_cover)
    expert_range = jnp.arange(EXPERTS, dtype=jnp.int32)
    in_window = expert_range % PER_INDEX < WAVE
    base = jax.random.randint(key_score, (TOK_DEV, EXPERTS), 0, 2 ** 16) * EXPERTS + expert_range[None, :]
    chosen_score = jnp.where(cover_full, 2 ** 30 + expert_range[None, :], -1 - expert_range[None, :])
    score = jnp.where(in_window[None, :], chosen_score, base)
    unused, picks = lax.top_k(score, TOP)
    order_keys = jax.random.randint(key_order, (TOK_DEV, TOP), 0, 2 ** 16) * TOP + jnp.arange(TOP, dtype=jnp.int32)[None, :]
    slot_order = jnp.argsort(order_keys, axis=1)
    return jnp.take_along_axis(picks, slot_order, axis=1).astype(jnp.int32)


def draw_expert_ids(key, part):
    blocks = jnp.arange(GROUPS * COLUMNS, dtype=jnp.int32)
    routed = jax.vmap(lambda block: block_routes(key, block))(blocks)
    return routed.reshape(TOKENS, TOP).astype(jnp.int32)


def block_scale(rng, shape, pieces, least, largest):
    gain, own = 1.0, jax.random.fold_in(rng, 6)
    for dim, blocks in pieces:
        heights = jnp.exp(jax.random.uniform(jax.random.fold_in(own, dim), (blocks,), jnp.float32, least / len(pieces), largest / len(pieces)))
        gain = gain * jnp.repeat(heights, shape[dim] // blocks).reshape([-1 if axis == dim else 1 for axis in range(len(shape))])
    return gain


def normal_values(stream_key, dims, spread, reach, cuts=(), kind=jnp.bfloat16):
    factor_of = block_scale(stream_key, dims, cuts, -0.22, 0.18) if cuts else 1.0
    values = jax.random.normal(stream_key, dims, jnp.float32) * spread * factor_of
    return jnp.minimum(jnp.maximum(values, -reach), reach).astype(kind)


def setup_inputs(seed: int = 0) -> dict:
    arg_keys = jax.random.split(jax.random.key(seed), 8)
    tokens = normal_values(arg_keys[0], (TOKENS, D), 1.0, 6.0, ((0, 32),))
    expert_ids = draw_expert_ids(jax.random.fold_in(arg_keys[7], 71), 0)
    gate_vals = jnp.clip(0.099609375 + 0.9003906 * jax.random.uniform(arg_keys[2], (TOKENS, TOP), jnp.float32) ** block_scale(arg_keys[2], (TOKENS, TOP), ((0, 32),), -0.2, 0.2), 0.099609375, 1.0).astype(jnp.bfloat16)
    w_gate = normal_values(arg_keys[3], (WINDOW, D, FF), D ** -0.5, 0.125, ((0, 4), (1, 8)))
    w_up = normal_values(arg_keys[4], (WINDOW, D, FF), D ** -0.5, 0.125, ((0, 4), (1, 8)))
    w_down = normal_values(arg_keys[5], (WINDOW, D, FF), FF ** -0.5, 0.15625, ((0, 4), (1, 8)))
    cotangent = normal_values(arg_keys[6], (TOKENS, D), 1.0, 6.0, ((0, 32),))
    return {"tokens": tokens, "expert_ids": expert_ids, "gate_vals": gate_vals, "w_gate": w_gate, "w_up": w_up, "w_down": w_down, "cotangent": cotangent}


def reference(tokens, expert_ids, gate_vals, w_gate, w_up, w_down, cotangent):
    slot_total = TOKENS * TOP
    model_width = tokens.shape[1]
    flat_ids = expert_ids.reshape(-1).astype(jnp.int32)
    local_index = flat_ids % PER_INDEX
    is_live = local_index < WAVE
    window_slot = jnp.where(is_live, (flat_ids // PER_INDEX) * WAVE + local_index, WINDOW).astype(jnp.int32)
    slot_ids = jnp.arange(slot_total, dtype=jnp.int32)
    column = ((slot_ids // TOP) // TOK_DEV) % COLUMNS
    zero_row = jnp.zeros((1, model_width), tokens.dtype)
    tokens_pad = jnp.concatenate([tokens, zero_row], axis=0)
    cot_pad = jnp.concatenate([cotangent, zero_row], axis=0)
    gate_pad = jnp.concatenate([gate_vals.reshape(-1), jnp.zeros((1,), gate_vals.dtype)], axis=0)
    capacity = GROUPS * MOST

    def pair_step(running, column_index, expert):
        out_acc, grad_acc, gate_acc, sum_gate, sum_up, sum_down = running
        chosen = (window_slot == expert) & (column == column_index)
        picked = jnp.nonzero(chosen, size=capacity, fill_value=slot_total)[0].astype(jnp.int32)
        token_at = (picked // TOP).astype(jnp.int32)
        row_data = tokens_pad[token_at]
        cot_rows = cot_pad[token_at]
        gate_rows = gate_pad[picked].astype(jnp.float32)
        weight_gate = w_gate[expert]
        weight_up = w_up[expert]
        weight_down = w_down[expert]
        gate_pre = jnp.dot(row_data, weight_gate, preferred_element_type=jnp.float32)
        up_pre = jnp.dot(row_data, weight_up, preferred_element_type=jnp.float32)
        sigmoid_g = jax.nn.sigmoid(gate_pre)
        hidden = (gate_pre * sigmoid_g * up_pre).astype(jnp.bfloat16)
        expert_out = jnp.dot(hidden, weight_down.T, preferred_element_type=jnp.float32).astype(jnp.bfloat16)
        out_f = expert_out.astype(jnp.float32)
        out_acc = out_acc.at[token_at].add(gate_rows[:, None] * out_f, mode="drop")
        gate_acc = gate_acc.at[picked].add(jnp.sum(cot_rows.astype(jnp.float32) * out_f, axis=1), mode="drop")
        out_grad = (gate_rows[:, None] * cot_rows.astype(jnp.float32)).astype(jnp.bfloat16)
        hidden_grad = jnp.dot(out_grad, weight_down, preferred_element_type=jnp.float32)
        gate_grad = (hidden_grad * up_pre * sigmoid_g * (1.0 + gate_pre * (1.0 - sigmoid_g))).astype(jnp.bfloat16)
        up_grad = (hidden_grad * gate_pre * sigmoid_g).astype(jnp.bfloat16)
        slot_grad = (jnp.dot(gate_grad, weight_gate.T, preferred_element_type=jnp.float32)
                     + jnp.dot(up_grad, weight_up.T, preferred_element_type=jnp.float32)).astype(jnp.bfloat16)
        grad_acc = grad_acc.at[token_at].add(slot_grad.astype(jnp.float32), mode="drop")
        part_gate = jnp.dot(row_data.T, gate_grad, preferred_element_type=jnp.float32).astype(jnp.bfloat16)
        part_up = jnp.dot(row_data.T, up_grad, preferred_element_type=jnp.float32).astype(jnp.bfloat16)
        part_down = jnp.dot(out_grad.T, hidden, preferred_element_type=jnp.float32).astype(jnp.bfloat16)
        sum_gate = sum_gate + part_gate.astype(jnp.float32)
        sum_up = sum_up + part_up.astype(jnp.float32)
        sum_down = sum_down + part_down.astype(jnp.float32)
        return (out_acc, grad_acc, gate_acc, sum_gate, sum_up, sum_down)

    def expert_step(running, expert):
        zeros_w = jnp.zeros((model_width, FF), jnp.float32)
        inside = (running[0], running[1], running[2], zeros_w, zeros_w, zeros_w)

        def column_step(state, column_index):
            return pair_step(state, column_index, expert), None

        inside, unused = lax.scan(column_step, inside, jnp.arange(COLUMNS, dtype=jnp.int32))
        return (inside[0], inside[1], inside[2]), (inside[3], inside[4], inside[5])

    initial = (jnp.zeros((TOKENS, model_width), jnp.float32),
               jnp.zeros((TOKENS, model_width), jnp.float32),
               jnp.zeros((slot_total,), jnp.float32))
    finished, weight_grads = lax.scan(expert_step, initial, jnp.arange(WINDOW, dtype=jnp.int32))
    output = finished[0].astype(jnp.bfloat16)
    grad_tokens = finished[1].astype(jnp.bfloat16)
    grad_gates = finished[2].reshape(TOKENS, TOP)
    return output, grad_tokens, grad_gates, weight_grads[0], weight_grads[1], weight_grads[2]
```

```python
import functools

import jax
import jax.numpy as jnp
from jax import lax
from jax.experimental import pallas as pl
from jax.experimental.pallas import tpu as pltpu
from jax.sharding import PartitionSpec as P

EXPERTS = 64
WAVE = 1
MOST = 48
F32 = jnp.float32
BF16 = jnp.bfloat16


def dot(a, b, dims):
    return lax.dot_general(a, b, (dims, ((), ())), preferred_element_type=F32)


MESH = pl.DeviceIdType.MESH
HBM = pl.BlockSpec(memory_space=pltpu.MemorySpace.HBM)
VMEM = pl.BlockSpec(memory_space=pltpu.MemorySpace.VMEM)


class Place:
    def __init__(self, groups):
        self.groups = groups
        self.e = lax.axis_index("expert")
        f = lax.axis_index("fsdp")
        self.f = f
        self.core = f % 2
        self.x, self.y = (f // 2) % 2, f // 4
        self.pair = f + 1 - 2 * self.core
        self.to_x, self.to_y = f + 2 - 4 * self.x, f + 4 - 8 * self.y

    def barrier(self):
        sem = pltpu.get_barrier_semaphore()
        peers = [(self.e, self.pair)]
        for step in range(self.groups):
            there = (self.e + step) % self.groups
            peers += [(there, self.to_x), (there, self.to_y)]
            if step:
                peers.append((there, self.f))
        for peer in peers:
            pl.semaphore_signal(sem, inc=1, device_id=peer, device_id_type=MESH)
        pl.semaphore_wait(sem, len(peers))


class Copies:
    def __init__(self, send, recv, local):
        self.sems = send, recv, local
        self.remote = self.near = 0
        self.pending = []

    def send(self, src, dst, to):
        send, recv, _ = self.sems
        copy = pltpu.make_async_remote_copy(
            src_ref=src,
            dst_ref=dst,
            send_sem=send.at[self.remote],
            recv_sem=recv.at[self.remote],
            device_id=to,
            device_id_type=MESH,
        )
        self.remote += 1
        copy.start()
        self.pending.append(copy)
        return copy

    def keep(self, src, dst):
        copy = pltpu.make_async_copy(src, dst, self.sems[2].at[self.near])
        self.near += 1
        copy.start()
        return copy


GATE, UP, DOWN = range(3)
REMOTE = 80
LOCAL = 16


def layer_kernel(groups, *refs):
    ws, (pick, weighted, tokens, cotangent) = refs[:3], refs[3:7]
    owns, output, grad_tokens, met = refs[7:10], refs[10], refs[11], refs[12]
    full, xs, rows_in, acc, pre_out, pre_in, act = refs[13:20]
    pair_out, pair_in, sum_out, near_in, back_out, back_in, far_acc = refs[20:27]
    at, go = Place(groups), Copies(*refs[27:30])
    block, ff = ws[0].shape
    rows = groups * MOST
    half_d = 4 * block
    piece = block // 2
    mine, pair = (at.e, at.f), (at.e, at.pair)
    across = [(at.e, at.to_y), (at.e, at.to_y), (at.e, at.to_x)]
    beside = [(at.e, at.to_x), (at.e, at.to_x), (at.e, at.to_y)]
    spot = [at.y, at.y, at.x]

    def span(q, s):
        return pl.ds(pl.multiple_of((2 * q + s) * block, block), block)

    def chip_span(q):
        return pl.ds(pl.multiple_of(2 * q * block, 2 * block), 2 * block)

    def part(start, size):
        return pl.ds(pl.multiple_of(start, piece), size)

    at.barrier()

    def fetch(m):
        copies = []
        for p in range(2):
            where = part((2 * spot[m] + at.core) * block + p * piece, piece)
            copies.append(
                go.send(ws[m].at[pl.ds(p * piece, piece)], full.at[m, where], across[m])
            )
        return copies

    def near(m):
        where = span(spot[m], at.core)
        return go.send(ws[m], full.at[m, where], pair), go.keep(ws[m], full.at[m, where])

    def forward(m, copies):
        out = []
        for p, copy in enumerate(copies):
            copy.wait_recv()
            where = full.at[m, part((2 * (1 - spot[m]) + at.core) * block + p * piece, piece)]
            out.append(go.send(where, where, pair))
        return out

    def spread(src, dst, other, half):
        copies = []
        for step in range(groups):
            there = (at.e + step) % groups
            if half == 0 and step == 0:
                copies.append(go.keep(src.at[0, at.e], dst.at[0, at.e]))
            else:
                copies.append(
                    go.send(src.at[half, there], dst.at[half, at.e], (there, other if half else at.f))
                )
        return copies

    def wait_in(copies):
        for copy in copies:
            if copy.is_remote:
                copy.wait_recv()
            else:
                copy.wait()

    def x_cols(half, k):
        x = 1 - at.x if half else at.x
        return pl.ds(pl.multiple_of((4 * k + 2 * x) * block, 2 * block), 2 * block)

    def y_cols(half):
        y = 1 - at.y if half else at.y
        return pl.ds(pl.multiple_of(4 * y * block, half_d), half_d)

    shape = (groups, MOST, -1)
    down_first = ((0,), (0,))
    plain, turned = ((1,), (0,)), ((1,), (1,))

    from_gate = fetch(GATE)
    near_gate = near(GATE)
    x_rows = []
    for half in (1, 0):
        for k in range(2):
            val = dot(pick[...], tokens[:, x_cols(half, k)], down_first).astype(BF16)
            xs[0, half, :, :, pl.ds(2 * k * block, 2 * block)] = val.reshape(shape[:2] + (2 * block,))
        x_rows += spread(xs.at[0], rows_in.at[0], at.to_x, half)
    from_up = fetch(UP)
    from_down = fetch(DOWN)
    near_up, near_down = near(UP), near(DOWN)
    og_rows = []
    for half in (1, 0):
        val = dot(weighted[...], cotangent[:, y_cols(half)], down_first).astype(BF16)
        xs[1, half] = val.reshape(shape[:2] + (half_d,))
        og_rows += spread(xs.at[1], rows_in.at[1], at.to_y, half)

    def lhs(t, cols):
        return rows_in[t, :, :, :, cols].reshape(2 * rows, -1)

    def begin(m, t):
        acc[m] = dot(lhs(t, chip_span(spot[m])), full[m, chip_span(spot[m])], plain)

    def finish(m, t):
        other = 1 - spot[m]
        acc[m] += dot(lhs(t, chip_span(other)), full[m, chip_span(other)], plain)
        pre_out[m] = acc[m, pl.ds(rows, rows)].astype(BF16)
        return go.send(pre_out.at[m], pre_in.at[m], beside[m])

    def wait_near(copies):
        copies[0].wait_recv()
        copies[1].wait()

    far_gate = forward(GATE, from_gate)
    wait_in(x_rows)
    wait_near(near_gate)
    begin(GATE, 0)
    wait_in(far_gate)
    pre_gate = finish(GATE, 0)
    wait_near(near_up)
    begin(UP, 0)
    far_down = forward(DOWN, from_down)
    far_up = forward(UP, from_up)
    wait_in(far_up)
    pre_up = finish(UP, 0)
    wait_near(near_down)
    wait_in(far_down)
    wait_in(og_rows)
    begin(DOWN, 1)
    pre_down = finish(DOWN, 1)

    tile = 16

    def hidden_rows(i, _):
        r = pl.ds(pl.multiple_of(i * tile, tile), tile)
        g = acc[GATE, r] + pre_in[GATE, r].astype(F32)
        u = acc[UP, r] + pre_in[UP, r].astype(F32)
        acc[GATE, r] = g
        acc[UP, r] = u
        act[DOWN, r] = (g * jax.nn.sigmoid(g) * u).astype(BF16)
        return 0

    def grad_rows(i, _):
        r = pl.ds(pl.multiple_of(i * tile, tile), tile)
        g, u = acc[GATE, r], acc[UP, r]
        h = acc[DOWN, r] + pre_in[DOWN, r].astype(F32)
        s = jax.nn.sigmoid(g)
        act[GATE, r] = (h * u * s * (1.0 + g * (1.0 - s))).astype(BF16)
        act[UP, r] = (h * g * s).astype(BF16)
        return 0

    top, low = pl.ds(0, rows), pl.ds(rows, rows)

    def share(m):
        return go.send(act.at[m, top], act.at[m, low], beside[m])

    pre_gate.wait_recv()
    pre_up.wait_recv()
    lax.fori_loop(0, rows // tile, hidden_rows, 0)
    got_hidden = share(DOWN)
    pre_down.wait_recv()
    lax.fori_loop(0, rows // tile, grad_rows, 0)
    got_gate = share(GATE)
    got_up = share(UP)

    def term(m, t, q, s):
        return dot(lhs(t, span(q, s)), act[m], down_first)

    def grads(m, t):
        q, other = spot[m], 1 - spot[m]
        pair_out[m, 0] = term(m, t, other, 1 - at.core).astype(BF16)
        to_far = go.send(pair_out.at[m, 0], pair_in.at[m, 0], pair)
        far_acc[...] = term(m, t, other, at.core)
        to_far.wait_recv()
        sum_out[m] = (far_acc[...] + pair_in[m, 0].astype(F32)).astype(BF16)
        to_other = go.send(sum_out.at[m], near_in.at[m], across[m])
        pair_out[m, 1] = term(m, t, q, 1 - at.core).astype(BF16)
        to_pair = go.send(pair_out.at[m, 1], pair_in.at[m, 1], pair)
        owns[m][...] = term(m, t, q, at.core)
        return to_other, to_pair

    got_hidden.wait_recv()
    back = []
    for half in (1, 0):
        hid = act[DOWN, low] if half else act[DOWN, top]
        back_out[0, half] = dot(hid, full[DOWN], turned).astype(BF16).reshape(shape[:2] + (half_d,))
        back += spread(back_out.at[0], back_in.at[0], at.to_y, half)
    got_gate.wait_recv()
    ends = [None] * 3
    ends[GATE] = grads(GATE, 0)
    got_up.wait_recv()
    back_grad = []
    for half in (1, 0):
        r = low if half else top
        val = dot(act[GATE, r], full[GATE], turned) + dot(act[UP, r], full[UP], turned)
        back_out[1, half] = val.astype(BF16).reshape(shape[:2] + (half_d,))
        back_grad += spread(back_out.at[1], back_in.at[1], at.to_x, half)
    ends[UP] = grads(UP, 0)
    ends[DOWN] = grads(DOWN, 1)

    wait_in(back)
    total = None
    for half in range(2):
        slot = back_in[0, half].reshape(rows, half_d)
        output[:, y_cols(half)] = dot(weighted[...], slot, plain).astype(BF16)
        val = dot(cotangent[:, y_cols(half)], slot, turned)
        total = val if total is None else total + val
    met[...] = total
    wait_in(back_grad)
    for half in range(2):
        for k in range(2):
            slot = back_in[1, half, :, :, pl.ds(2 * k * block, 2 * block)].reshape(rows, 2 * block)
            grad_tokens[:, x_cols(half, k)] = dot(pick[...], slot, plain).astype(BF16)
    for m in (GATE, DOWN, UP):
        to_other, to_pair = ends[m]
        to_pair.wait_recv()
        to_other.wait_recv()
        owns[m][...] += pair_in[m, 1].astype(F32) + near_in[m].astype(F32)
    for copy in go.pending:
        copy.wait_send()


def layer_call(groups, ws, pick, weighted, tokens, cotangent):
    dma = pltpu.SemaphoreType.DMA
    block, ff = ws[0].shape
    tok, width = tokens.shape
    rows = groups * MOST
    wide = (2, 2, groups, MOST, width // 2)
    vmem = pltpu.VMEM
    return pl.pallas_call(
        functools.partial(layer_kernel, groups),
        out_shape=[jax.ShapeDtypeStruct((block, ff), F32)] * 3
        + [jax.ShapeDtypeStruct((tok, width), BF16)] * 2
        + [jax.ShapeDtypeStruct((tok, rows), F32)],
        in_specs=[HBM] * 3 + [VMEM] * 4,
        out_specs=[VMEM] * 6,
        scratch_shapes=[
            vmem((3, 4 * block, ff), BF16),
            vmem(wide, BF16),
            vmem(wide, BF16),
            vmem((3, 2 * rows, ff), F32),
            vmem((3, rows, ff), BF16),
            vmem((3, rows, ff), BF16),
            vmem((3, 2 * rows, ff), BF16),
            vmem((3, 2, block, ff), BF16),
            vmem((3, 2, block, ff), BF16),
            vmem((3, block, ff), BF16),
            vmem((3, block, ff), BF16),
            vmem(wide, BF16),
            vmem(wide, BF16),
            vmem((block, ff), F32),
            dma((REMOTE,)),
            dma((REMOTE,)),
            dma((LOCAL,)),
        ],
        compiler_params=pltpu.CompilerParams(
            collective_id=0, has_side_effects=True, vmem_limit_bytes=62 * 2**20
        ),
    )(*ws, pick, weighted, tokens, cotangent)


def routes(expert_ids, gate_vals, groups):
    per_index = EXPERTS // groups
    window = WAVE * groups
    tok_count = expert_ids.shape[0]
    local_index = expert_ids % per_index
    window_slot = jnp.where(
        local_index < WAVE, expert_ids // per_index * WAVE + local_index, window
    )
    slot_is = window_slot[:, :, None] == jnp.arange(window, dtype=jnp.int32)[None, None, :]
    chosen = jnp.any(slot_is, axis=1)
    gate_of = jnp.sum(jnp.where(slot_is, gate_vals.astype(F32)[:, :, None], 0.0), axis=1)
    tok = jnp.arange(tok_count, dtype=jnp.int32)
    before = (tok[:, None] > tok[None, :]).astype(BF16)
    rank = dot(before, chosen.astype(BF16), ((1,), (0,))).astype(jnp.int32)
    place = chosen[:, :, None] & (
        rank[:, :, None] == jnp.arange(MOST, dtype=jnp.int32)[None, None, :]
    )
    pick = place.astype(BF16).reshape(tok_count, window * MOST)
    weighted = (
        jnp.where(place, gate_of[:, :, None], 0.0).astype(BF16).reshape(tok_count, window * MOST)
    )
    return slot_is, place, pick, weighted


def on_device(tokens, expert_ids, gate_vals, w_gate, w_up, w_down, cotangent):
    groups = lax.axis_size("expert")
    columns = lax.axis_size("fsdp")
    side = lax.axis_index("fsdp") % 2
    tok_count, width = tokens.shape
    block = w_gate.shape[1]
    rows = groups * MOST
    sides = [[i for i in range(columns) if i % 2 == s] for s in (0, 1)]
    pairs = [(i, i ^ 1) for i in range(columns)]

    def swap(x):
        return lax.ppermute(x, "fsdp", pairs)

    def gather(w):
        return lax.all_gather(w[0], "fsdp", axis_index_groups=sides, axis=0, tiled=True)

    def scatter(x):
        return lax.psum_scatter(
            x.astype(BF16), "fsdp", scatter_dimension=0, axis_index_groups=sides, tiled=True
        ).astype(F32)[None]

    def cut(x, odd):
        return jnp.concatenate(
            [x[:, (2 * k + odd) * block : (2 * k + odd + 1) * block] for k in range(columns // 2)],
            axis=1,
        )

    def halves(x):
        even, odd = cut(x, 0), cut(x, 1)
        return jnp.where(side == 0, even, odd), jnp.where(side == 0, odd, even)

    def whole_rows(mine, other):
        even, odd = jnp.where(side == 0, mine, other), jnp.where(side == 0, other, mine)
        parts = []
        for k in range(columns // 2):
            here = slice(k * block, (k + 1) * block)
            parts += [even[:, here], odd[:, here]]
        return jnp.concatenate(parts, axis=1)

    def exchange(mine, other):
        packed = jnp.stack(
            [mine.reshape(groups, MOST, width // 2), other.reshape(groups, MOST, width // 2)],
            axis=1,
        )
        there = lax.all_to_all(packed, "expert", split_axis=0, concat_axis=0, tiled=True)
        return there[:, 0].reshape(rows, width // 2), there[:, 1].reshape(rows, width // 2)

    square = columns == 8
    slot_is, place, pick, weighted = routes(expert_ids, gate_vals, groups)
    first = ((0,), (0,))
    if square:
        *grad_w, output, grad_tokens, met = layer_call(
            groups, [w_gate[0], w_up[0], w_down[0]], pick, weighted, tokens, cotangent
        )
        met = jnp.sum(jnp.where(place, met.reshape(place.shape), 0.0), axis=2)
        grad_gates = jnp.sum(jnp.where(slot_is, met[:, None, :], 0.0), axis=2)
        return (output, grad_tokens, grad_gates, *(g[None] for g in grad_w))
    full_gate, full_up, full_down = gather(w_gate), gather(w_up), gather(w_down)
    row_mine, row_other = exchange(*halves(dot(pick, tokens, first).astype(BF16)))
    og_mine, og_other = exchange(*halves(dot(weighted, cotangent, first).astype(BF16)))
    row_in = jnp.concatenate([row_mine, swap(row_other)], axis=0)
    out_grad = jnp.concatenate([og_mine, swap(og_other)], axis=0)

    def summed(x):
        return x[:rows] + swap(x[rows:].astype(BF16)).astype(F32)

    def both(x):
        return jnp.concatenate([x, swap(x)], axis=0)

    plain, turned = ((1,), (0,)), ((1,), (1,))
    gate_pre = summed(dot(row_in, full_gate, plain))
    up_pre = summed(dot(row_in, full_up, plain))
    sigmoid_g = jax.nn.sigmoid(gate_pre)
    hidden = (gate_pre * sigmoid_g * up_pre).astype(BF16)
    hidden_grad = summed(dot(out_grad, full_down, plain))
    gate_grad = (
        hidden_grad * up_pre * sigmoid_g * (1.0 + gate_pre * (1.0 - sigmoid_g))
    ).astype(BF16)
    up_grad = (hidden_grad * gate_pre * sigmoid_g).astype(BF16)
    hidden, gate_grad, up_grad = both(hidden), both(gate_grad), both(up_grad)
    grad_w_down = scatter(dot(out_grad, hidden, first))
    grad_w_gate = scatter(dot(row_in, gate_grad, first))
    grad_w_up = scatter(dot(row_in, up_grad, first))
    expert_out = dot(hidden, full_down, turned).astype(BF16)
    slot_grad = (dot(gate_grad, full_gate, turned) + dot(up_grad, full_up, turned)).astype(BF16)
    outs = exchange(expert_out[:rows], swap(expert_out[rows:]))
    grads = exchange(slot_grad[:rows], swap(slot_grad[rows:]))

    slot_out = whole_rows(*outs)
    output = dot(weighted, slot_out, plain).astype(BF16)
    grad_tokens = dot(pick, whole_rows(*grads), plain).astype(BF16)
    met = dot(cotangent, slot_out, turned)
    met = jnp.sum(jnp.where(place, met.reshape(place.shape), 0.0), axis=2)
    grad_gates = jnp.sum(jnp.where(slot_is, met[:, None, :], 0.0), axis=2)
    return (output, grad_tokens, grad_gates, grad_w_gate, grad_w_up, grad_w_down)


def solution(mesh):
    token = P(("expert", "fsdp"), None)
    weight = P("expert", "fsdp", None)
    return jax.shard_map(
        on_device,
        mesh=mesh,
        in_specs=(token, token, token, weight, weight, weight, token),
        out_specs=(token, token, token, weight, weight, weight),
        check_vma=False,
    )
```

```python
import functools

import jax
import jax.numpy as jnp
from jax import lax
from jax.experimental import pallas as pl
from jax.experimental.pallas import tpu as pltpu
from jax.sharding import PartitionSpec as P

EXPERTS = 64
WAVE = 1
MOST = 48
F32 = jnp.float32
BF16 = jnp.bfloat16


def dot(a, b, dims):
    return lax.dot_general(a, b, (dims, ((), ())), preferred_element_type=F32)


MESH = pl.DeviceIdType.MESH
HBM = pl.BlockSpec(memory_space=pltpu.MemorySpace.HBM)
VMEM = pl.BlockSpec(memory_space=pltpu.MemorySpace.VMEM)


class Place:
    def __init__(self, groups):
        self.groups = groups
        self.e = lax.axis_index("expert")
        f = lax.axis_index("fsdp")
        self.f = f
        self.core = f % 2
        self.x, self.y = (f // 2) % 2, f // 4
        self.pair = f + 1 - 2 * self.core
        self.to_x, self.to_y = f + 2 - 4 * self.x, f + 4 - 8 * self.y

    def barrier(self):
        sem = pltpu.get_barrier_semaphore()
        peers = [(self.e, self.pair)]
        for step in range(self.groups):
            there = (self.e + step) % self.groups
            peers += [(there, self.to_x), (there, self.to_y)]
            if step:
                peers.append((there, self.f))
        for peer in peers:
            pl.semaphore_signal(sem, inc=1, device_id=peer, device_id_type=MESH)
        pl.semaphore_wait(sem, len(peers))


class Copies:
    def __init__(self, send, recv, local):
        self.sems = send, recv, local
        self.remote = self.near = 0
        self.pending = []

    def send(self, src, dst, to):
        send, recv, _ = self.sems
        copy = pltpu.make_async_remote_copy(
            src_ref=src,
            dst_ref=dst,
            send_sem=send.at[self.remote],
            recv_sem=recv.at[self.remote],
            device_id=to,
            device_id_type=MESH,
        )
        self.remote += 1
        copy.start()
        self.pending.append(copy)
        return copy

    def drain(self, copies):
        ids = {id(copy) for copy in copies}
        for copy in self.pending:
            if id(copy) in ids:
                copy.wait_send()
        self.pending = [copy for copy in self.pending if id(copy) not in ids]

    def keep(self, src, dst):
        copy = pltpu.make_async_copy(src, dst, self.sems[2].at[self.near])
        self.near += 1
        copy.start()
        return copy


GATE, UP, DOWN = range(3)
REMOTE = 128
LOCAL = 16


def chunks(ff):
    lanes = 128
    first = (ff // lanes + 1) // 2 * lanes
    return [pl.ds(0, first), pl.ds(first, ff - first)]


def route(groups, ids, gates):
    tok = ids.shape[1]
    rows = groups * MOST
    per_index = EXPERTS // groups
    slot = lax.broadcasted_iota(jnp.int32, (rows, tok), 0)
    target, place_in = jnp.zeros_like(slot), slot
    for g in range(1, groups):
        later = slot >= g * MOST
        target = target + jnp.where(later, per_index, 0)
        place_in = place_in - jnp.where(later, MOST, 0)
    chosen, gate_of = None, None
    vals = gates[...].astype(F32)
    for k in range(ids.shape[0]):
        hit = ids[pl.ds(k, 1), :] == target
        val = jnp.where(hit, vals[k : k + 1, :], 0.0)
        one = jnp.where(hit, 1.0, 0.0)
        chosen = one if chosen is None else chosen + one
        gate_of = val if gate_of is None else gate_of + val
    earlier = lax.broadcasted_iota(jnp.int32, (tok, tok), 0) < lax.broadcasted_iota(
        jnp.int32, (tok, tok), 1
    )
    rank = dot(chosen.astype(BF16), jnp.where(earlier, 1.0, 0.0).astype(BF16), ((1,), (0,)))
    place = (chosen > 0.0) & (rank == place_in.astype(F32))
    return (
        target,
        jnp.where(place, 1.0, 0.0).astype(BF16),
        jnp.where(place, gate_of, 0.0).astype(BF16),
    )


def layer_kernel(groups, *refs):
    ws, arrays_in = refs[:3], refs[3:7]
    owns, output, grad_tokens, grad_gates = refs[7:10], refs[10], refs[11], refs[12]
    full, xs, rows_in, acc, pre_out, pre_in, act = refs[13:20]
    pair_out, pair_in, near_in, back_in = refs[20:24]
    ids, gates, tokens, cotangent, pick, weighted = arrays = refs[24:30]
    at, go = Place(groups), Copies(*refs[30:33])
    block, ff = ws[0].shape
    rows = groups * MOST
    half_d = 4 * block
    cuts = chunks(ff)
    pair = (at.e, at.pair)
    across = [(at.e, at.to_y), (at.e, at.to_y), (at.e, at.to_x)]
    beside = [(at.e, at.to_x), (at.e, at.to_x), (at.e, at.to_y)]
    spot = [at.y, at.y, at.x]
    shape = (groups, MOST)
    first = ((0,), (0,))
    plain, turned = ((1,), (0,)), ((1,), (1,))
    top, low = pl.ds(0, rows), pl.ds(rows, rows)

    def span(q, s):
        return pl.ds(pl.multiple_of((2 * q + s) * block, block), block)

    def chip_span(q):
        return pl.ds(pl.multiple_of(2 * q * block, 2 * block), 2 * block)

    def fetch(m, c):
        return go.send(ws[m].at[:, c], full.at[m, span(spot[m], at.core), c], across[m])

    def near(m, c):
        where = full.at[m, span(spot[m], at.core), c]
        return [go.send(ws[m].at[:, c], where, pair), go.keep(ws[m].at[:, c], where)]

    def forward(m, c, copy):
        copy.wait_recv()
        where = full.at[m, span(1 - spot[m], at.core), c]
        return go.send(where, where, pair)

    def spread(src, dst, other, half):
        copies = []
        for step in range(groups):
            there = (at.e + step) % groups
            if half == 0 and step == 0:
                copies.append(go.keep(src.at[0, at.e], dst.at[0, at.e]))
            else:
                to = (there, other if half else at.f)
                copies.append(go.send(src.at[half, there], dst.at[half, at.e], to))
        return copies

    def wait_in(copies):
        for copy in copies:
            if copy.is_remote:
                copy.wait_recv()
            else:
                copy.wait()

    def x_cols(half, k):
        x = 1 - at.x if half else at.x
        return pl.ds(pl.multiple_of((4 * k + 2 * x) * block, 2 * block), 2 * block)

    def y_cols(half):
        y = 1 - at.y if half else at.y
        return pl.ds(pl.multiple_of(4 * y * block, half_d), half_d)

    loads = [go.keep(src, dst) for src, dst in zip(arrays_in, arrays)]
    at.barrier()
    coming = {}
    nearby = {}
    for m in (GATE, UP):
        coming[m, 0] = fetch(m, cuts[0])
    for m in (GATE, UP):
        nearby[m, 0] = near(m, cuts[0])
    wait_in(loads[:2])
    target, pick_val, weighted_val = route(groups, ids, gates)
    pick[...] = pick_val
    weighted[...] = weighted_val
    loads[2].wait()
    x_rows, og_rows = [], []
    for half in (1, 0):
        for k in range(2):
            val = dot(pick[...], tokens[:, x_cols(half, k)], plain).astype(BF16)
            xs[0, half, :, :, pl.ds(2 * k * block, 2 * block)] = val.reshape(shape + (2 * block,))
        x_rows += spread(xs.at[0], rows_in.at[0], at.to_x, half)
    for c in range(2):
        coming[DOWN, c] = fetch(DOWN, cuts[c])
    loads[3].wait()
    for half in (1, 0):
        val = dot(weighted[...], cotangent[:, y_cols(half)], plain).astype(BF16)
        xs[1, half] = val.reshape(shape + (half_d,))
        og_rows += spread(xs.at[1], rows_in.at[1], at.to_y, half)
    for m in (GATE, UP):
        coming[m, 1] = fetch(m, cuts[1])
    for m, c in ((DOWN, 0), (DOWN, 1), (GATE, 1), (UP, 1)):
        nearby[m, c] = near(m, cuts[c])

    def lhs(t, cols):
        return rows_in[t, :, :, :, cols].reshape(2 * rows, -1)

    def begin(m, t, c):
        wait_in(nearby[m, c])
        cut, where = cuts[c], chip_span(spot[m])
        acc[m, :, cut] = dot(lhs(t, where), full[m, where, cut], plain)

    def finish(m, t, c, far):
        far.wait_recv()
        cut, where = cuts[c], chip_span(1 - spot[m])
        acc[m, :, cut] += dot(lhs(t, where), full[m, where, cut], plain)
        pre_out[m, top, cut] = acc[m, low, cut].astype(BF16)
        return go.send(pre_out.at[m, top, cut], pre_in.at[m, :, cut], beside[m])

    tile = 16

    def make_hidden(c):
        cut = cuts[c]

        def body(i, _):
            r = pl.ds(pl.multiple_of(i * tile, tile), tile)
            g = acc[GATE, r, cut] + pre_in[GATE, r, cut].astype(F32)
            u = acc[UP, r, cut] + pre_in[UP, r, cut].astype(F32)
            acc[GATE, r, cut] = g
            acc[UP, r, cut] = u
            act[DOWN, r, cut] = (g * jax.nn.sigmoid(g) * u).astype(BF16)
            return 0

        lax.fori_loop(0, rows // tile, body, 0)

    def make_grads(c):
        cut = cuts[c]

        def body(i, _):
            r = pl.ds(pl.multiple_of(i * tile, tile), tile)
            g, u = acc[GATE, r, cut], acc[UP, r, cut]
            h = acc[DOWN, r, cut] + pre_in[DOWN, r, cut].astype(F32)
            s = jax.nn.sigmoid(g)
            act[GATE, r, cut] = (h * u * s * (1.0 + g * (1.0 - s))).astype(BF16)
            act[UP, r, cut] = (h * g * s).astype(BF16)
            return 0

        lax.fori_loop(0, rows // tile, body, 0)

    def share(m, c):
        return go.send(act.at[m, top, cuts[c]], act.at[m, low, cuts[c]], beside[m])

    ends = []
    back_out = xs

    def grads(m, t, c):
        cut, q, other = cuts[c], spot[m], 1 - spot[m]

        def term(q, s):
            return dot(lhs(t, span(q, s)), act[m, :, cut], first)

        pair_out[m, 0, :, cut] = term(other, 1 - at.core).astype(BF16)
        to_far = go.send(pair_out.at[m, 0, :, cut], pair_in.at[m, 0, :, cut], pair)
        acc[m, pl.ds(0, block), cut] = term(other, at.core)
        pair_out[m, 1, :, cut] = term(q, 1 - at.core).astype(BF16)
        to_pair = go.send(pair_out.at[m, 1, :, cut], pair_in.at[m, 1, :, cut], pair)
        to_far.wait_recv()
        both = acc[m, pl.ds(0, block), cut] + pair_in[m, 0, :, cut].astype(F32)
        pre_out[m, :, cut] = both.astype(BF16)
        to_other = go.send(pre_out.at[m, :, cut], near_in.at[m, :, cut], across[m])
        owns[m][:, cut] = term(q, at.core)
        ends.append((m, c, to_other, to_pair))

    pre, got = {}, {}
    far = {(m, 0): forward(m, cuts[0], coming[m, 0]) for m in (GATE, UP)}
    wait_in(x_rows)
    for m in (GATE, UP):
        begin(m, 0, 0)
    for m in (GATE, UP):
        pre[m, 0] = finish(m, 0, 0, far[m, 0])
    for c in range(2):
        far[DOWN, c] = forward(DOWN, cuts[c], coming[DOWN, c])
    for m in (GATE, UP):
        begin(m, 0, 1)
    far[GATE, 1] = forward(GATE, cuts[1], coming[GATE, 1])
    wait_in(og_rows)
    for c in range(2):
        begin(DOWN, 1, c)
        pre[DOWN, c] = finish(DOWN, 1, c, far[DOWN, c])
    pre[GATE, 0].wait_recv()
    pre[UP, 0].wait_recv()
    make_hidden(0)
    got[DOWN, 0] = share(DOWN, 0)
    pre[GATE, 1] = finish(GATE, 0, 1, far[GATE, 1])
    far[UP, 1] = forward(UP, cuts[1], coming[UP, 1])
    pre[UP, 1] = finish(UP, 0, 1, far[UP, 1])
    pre[DOWN, 0].wait_recv()
    make_grads(0)
    for m in (GATE, UP):
        got[m, 0] = share(m, 0)
    pre[GATE, 1].wait_recv()
    pre[UP, 1].wait_recv()
    make_hidden(1)
    got[DOWN, 1] = share(DOWN, 1)
    pre[DOWN, 1].wait_recv()
    make_grads(1)
    for m in (GATE, UP):
        got[m, 1] = share(m, 1)

    go.drain(list(pre.values()) + x_rows + og_rows)
    got[GATE, 0].wait_recv()
    grads(GATE, 0, 0)
    got[DOWN, 0].wait_recv()
    got[DOWN, 1].wait_recv()
    back_out[0] = dot(act[DOWN], full[DOWN], turned).astype(BF16).reshape((2,) + shape + (half_d,))
    back, back_grad = [], []
    for half in (1, 0):
        back += spread(back_out.at[0], back_in.at[0], at.to_y, half)
    got[UP, 0].wait_recv()
    grads(UP, 0, 0)
    grads(DOWN, 1, 0)
    got[GATE, 1].wait_recv()
    got[UP, 1].wait_recv()
    slot_grad = dot(act[GATE], full[GATE], turned) + dot(act[UP], full[UP], turned)
    back_out[1] = slot_grad.astype(BF16).reshape((2,) + shape + (half_d,))
    for half in (1, 0):
        back_grad += spread(back_out.at[1], back_in.at[1], at.to_x, half)
    grads(GATE, 0, 1)
    grads(UP, 0, 1)
    grads(DOWN, 1, 1)

    wait_in(back)
    met = None
    for half in range(2):
        slot = back_in[0, half].reshape(rows, half_d)
        output[:, y_cols(half)] = dot(weighted[...], slot, first).astype(BF16)
        val = dot(slot, cotangent[:, y_cols(half)], turned)
        met = val if met is None else met + val
    met = jnp.where(pick[...].astype(F32) > 0.0, met, 0.0)
    for k in range(ids.shape[0]):
        hit = jnp.where(ids[pl.ds(k, 1), :] == target, met, 0.0)
        grad_gates[pl.ds(k, 1), :] = jnp.sum(hit, axis=0, keepdims=True)
    wait_in(back_grad)
    for half in range(2):
        for k in range(2):
            slot = back_in[1, half, :, :, pl.ds(2 * k * block, 2 * block)].reshape(rows, 2 * block)
            grad_tokens[:, x_cols(half, k)] = dot(pick[...], slot, first).astype(BF16)
    for m, c, to_other, to_pair in ends:
        cut = cuts[c]
        to_pair.wait_recv()
        to_other.wait_recv()
        owns[m][:, cut] += pair_in[m, 1, :, cut].astype(F32) + near_in[m, :, cut].astype(F32)
    go.drain(go.pending)


def stay(x):
    return pltpu.with_memory_space_constraint(x, pltpu.MemorySpace.HBM)


def layer_call(groups, ws, ids, gates, tokens, cotangent):
    dma = pltpu.SemaphoreType.DMA
    block, ff = ws[0].shape
    tok, width = tokens.shape
    rows = groups * MOST
    wide = (2, 2, groups, MOST, width // 2)
    vmem = pltpu.VMEM
    return pl.pallas_call(
        functools.partial(layer_kernel, groups),
        out_shape=[jax.ShapeDtypeStruct((block, ff), F32)] * 3
        + [jax.ShapeDtypeStruct((tok, width), BF16)] * 2
        + [jax.ShapeDtypeStruct(ids.shape, F32)],
        in_specs=[HBM] * 7,
        out_specs=[VMEM] * 6,
        scratch_shapes=[
            vmem((3, 4 * block, ff), BF16),
            vmem(wide, BF16),
            vmem(wide, BF16),
            vmem((3, 2 * rows, ff), F32),
            vmem((3, block, ff), BF16),
            vmem((3, rows, ff), BF16),
            vmem((3, 2 * rows, ff), BF16),
            vmem((3, 2, block, ff), BF16),
            vmem((3, 2, block, ff), BF16),
            vmem((3, block, ff), BF16),
            vmem(wide, BF16),
            vmem(ids.shape, ids.dtype),
            vmem(gates.shape, gates.dtype),
            vmem((tok, width), BF16),
            vmem((tok, width), BF16),
            vmem((rows, tok), BF16),
            vmem((rows, tok), BF16),
            dma((REMOTE,)),
            dma((REMOTE,)),
            dma((LOCAL,)),
        ],
        compiler_params=pltpu.CompilerParams(
            collective_id=0, has_side_effects=True, vmem_limit_bytes=41 * 2**20
        ),
    )(*map(stay, [*ws, ids, gates, tokens, cotangent]))


def store_kernel(*refs):
    n = len(refs) // 2
    srcs, dsts, sems = refs[:n], refs[n : 2 * n], refs[2 * n]
    copies = [pltpu.make_async_copy(srcs[i], dsts[i], sems.at[i]) for i in range(n)]
    for copy in copies:
        copy.start()
    for copy in copies:
        copy.wait()


def store_call(arrays):
    return pl.pallas_call(
        store_kernel,
        out_shape=[jax.ShapeDtypeStruct(a.shape, a.dtype) for a in arrays],
        in_specs=[VMEM] * len(arrays),
        out_specs=[HBM] * len(arrays),
        scratch_shapes=[pltpu.SemaphoreType.DMA((len(arrays),))],
        compiler_params=pltpu.CompilerParams(vmem_limit_bytes=2**20),
    )(*arrays)


def routes(expert_ids, gate_vals, groups):
    per_index = EXPERTS // groups
    window = WAVE * groups
    tok_count = expert_ids.shape[0]
    local_index = expert_ids % per_index
    window_slot = jnp.where(
        local_index < WAVE, expert_ids // per_index * WAVE + local_index, window
    )
    slot_is = window_slot[:, :, None] == jnp.arange(window, dtype=jnp.int32)[None, None, :]
    chosen = jnp.any(slot_is, axis=1)
    gate_of = jnp.sum(jnp.where(slot_is, gate_vals.astype(F32)[:, :, None], 0.0), axis=1)
    tok = jnp.arange(tok_count, dtype=jnp.int32)
    before = (tok[:, None] > tok[None, :]).astype(BF16)
    rank = dot(before, chosen.astype(BF16), ((1,), (0,))).astype(jnp.int32)
    place = chosen[:, :, None] & (
        rank[:, :, None] == jnp.arange(MOST, dtype=jnp.int32)[None, None, :]
    )
    pick = place.astype(BF16).reshape(tok_count, window * MOST)
    weighted = (
        jnp.where(place, gate_of[:, :, None], 0.0).astype(BF16).reshape(tok_count, window * MOST)
    )
    return slot_is, place, pick, weighted


def on_device(tokens, expert_ids, gate_vals, w_gate, w_up, w_down, cotangent):
    groups = lax.axis_size("expert")
    columns = lax.axis_size("fsdp")
    side = lax.axis_index("fsdp") % 2
    tok_count, width = tokens.shape
    block = w_gate.shape[1]
    rows = groups * MOST
    sides = [[i for i in range(columns) if i % 2 == s] for s in (0, 1)]
    pairs = [(i, i ^ 1) for i in range(columns)]

    def swap(x):
        return lax.ppermute(x, "fsdp", pairs)

    def gather(w):
        return lax.all_gather(w[0], "fsdp", axis_index_groups=sides, axis=0, tiled=True)

    def scatter(x):
        return lax.psum_scatter(
            x.astype(BF16), "fsdp", scatter_dimension=0, axis_index_groups=sides, tiled=True
        ).astype(F32)[None]

    def cut(x, odd):
        return jnp.concatenate(
            [x[:, (2 * k + odd) * block : (2 * k + odd + 1) * block] for k in range(columns // 2)],
            axis=1,
        )

    def halves(x):
        even, odd = cut(x, 0), cut(x, 1)
        return jnp.where(side == 0, even, odd), jnp.where(side == 0, odd, even)

    def whole_rows(mine, other):
        even, odd = jnp.where(side == 0, mine, other), jnp.where(side == 0, other, mine)
        parts = []
        for k in range(columns // 2):
            here = slice(k * block, (k + 1) * block)
            parts += [even[:, here], odd[:, here]]
        return jnp.concatenate(parts, axis=1)

    def exchange(mine, other):
        packed = jnp.stack(
            [mine.reshape(groups, MOST, width // 2), other.reshape(groups, MOST, width // 2)],
            axis=1,
        )
        there = lax.all_to_all(packed, "expert", split_axis=0, concat_axis=0, tiled=True)
        return there[:, 0].reshape(rows, width // 2), there[:, 1].reshape(rows, width // 2)

    square = columns == 8
    first = ((0,), (0,))
    if square:
        results = layer_call(
            groups, [w_gate[0], w_up[0], w_down[0]], expert_ids.T, gate_vals.T, tokens, cotangent
        )
        *grad_w, output, grad_tokens, grad_gates = store_call(results)
        return (output, grad_tokens, grad_gates.T, *(g[None] for g in grad_w))
    slot_is, place, pick, weighted = routes(expert_ids, gate_vals, groups)
    full_gate, full_up, full_down = gather(w_gate), gather(w_up), gather(w_down)
    row_mine, row_other = exchange(*halves(dot(pick, tokens, first).astype(BF16)))
    og_mine, og_other = exchange(*halves(dot(weighted, cotangent, first).astype(BF16)))
    row_in = jnp.concatenate([row_mine, swap(row_other)], axis=0)
    out_grad = jnp.concatenate([og_mine, swap(og_other)], axis=0)

    def summed(x):
        return x[:rows] + swap(x[rows:].astype(BF16)).astype(F32)

    def both(x):
        return jnp.concatenate([x, swap(x)], axis=0)

    plain, turned = ((1,), (0,)), ((1,), (1,))
    gate_pre = summed(dot(row_in, full_gate, plain))
    up_pre = summed(dot(row_in, full_up, plain))
    sigmoid_g = jax.nn.sigmoid(gate_pre)
    hidden = (gate_pre * sigmoid_g * up_pre).astype(BF16)
    hidden_grad = summed(dot(out_grad, full_down, plain))
    gate_grad = (
        hidden_grad * up_pre * sigmoid_g * (1.0 + gate_pre * (1.0 - sigmoid_g))
    ).astype(BF16)
    up_grad = (hidden_grad * gate_pre * sigmoid_g).astype(BF16)
    hidden, gate_grad, up_grad = both(hidden), both(gate_grad), both(up_grad)
    grad_w_down = scatter(dot(out_grad, hidden, first))
    grad_w_gate = scatter(dot(row_in, gate_grad, first))
    grad_w_up = scatter(dot(row_in, up_grad, first))
    expert_out = dot(hidden, full_down, turned).astype(BF16)
    slot_grad = (dot(gate_grad, full_gate, turned) + dot(up_grad, full_up, turned)).astype(BF16)
    outs = exchange(expert_out[:rows], swap(expert_out[rows:]))
    grads = exchange(slot_grad[:rows], swap(slot_grad[rows:]))

    slot_out = whole_rows(*outs)
    output = dot(weighted, slot_out, plain).astype(BF16)
    grad_tokens = dot(pick, whole_rows(*grads), plain).astype(BF16)
    met = dot(cotangent, slot_out, turned)
    met = jnp.sum(jnp.where(place, met.reshape(place.shape), 0.0), axis=2)
    grad_gates = jnp.sum(jnp.where(slot_is, met[:, None, :], 0.0), axis=2)
    return (output, grad_tokens, grad_gates, grad_w_gate, grad_w_up, grad_w_down)


def solution(mesh):
    token = P(("expert", "fsdp"), None)
    weight = P("expert", "fsdp", None)
    return jax.shard_map(
        on_device,
        mesh=mesh,
        in_specs=(token, token, token, weight, weight, weight, token),
        out_specs=(token, token, token, weight, weight, weight),
        check_vma=False,
    )
```

```python
import functools

import jax
import jax.numpy as jnp
from jax import lax
from jax.experimental import pallas as pl
from jax.experimental.pallas import tpu as pltpu
from jax.sharding import PartitionSpec as P

EXPERTS = 64
WAVE = 1
MOST = 48
F32 = jnp.float32
BF16 = jnp.bfloat16


def dot(a, b, dims):
    return lax.dot_general(a, b, (dims, ((), ())), preferred_element_type=F32)


MESH = pl.DeviceIdType.MESH
HBM = pl.BlockSpec(memory_space=pltpu.MemorySpace.HBM)
VMEM = pl.BlockSpec(memory_space=pltpu.MemorySpace.VMEM)


class Place:
    def __init__(self, groups):
        self.groups = groups
        self.e = lax.axis_index("expert")
        f = lax.axis_index("fsdp")
        self.f = f
        self.core = f % 2
        self.x, self.y = (f // 2) % 2, f // 4
        self.pair = f + 1 - 2 * self.core
        self.others = [3 - self.e, (self.e + 2) % 4, self.e + 1 - 2 * (self.e % 2)]
        self.to_x, self.to_y = f + 2 - 4 * self.x, f + 4 - 8 * self.y

    def planes(self):
        return [(1, self.others[2]), (3, self.others[0]), (2, self.others[1]), (0, self.e)]

    def tell(self, sem, e, f):
        pl.semaphore_signal(sem, inc=1, device_id=(e, f), device_id_type=MESH)

    def enter_plane(self, plane_sem):
        sem = pltpu.get_barrier_semaphore()
        self.tell(sem, self.e, self.to_x - self.core)
        self.tell(sem, self.e, self.to_y - self.core)

        @pl.when(self.core == 1)
        def _():
            self.tell(sem, self.e, self.pair)

        @pl.when(self.core == 0)
        def _():
            pl.semaphore_wait(sem, 5)
            self.tell(plane_sem, self.e, self.pair)

        @pl.when(self.core == 1)
        def _():
            pl.semaphore_wait(plane_sem, 1)
            for there in self.others:
                self.tell(sem, there, self.f)

    def enter_slice(self, slice_sem):
        @pl.when(self.core == 1)
        def _():
            pl.semaphore_wait(pltpu.get_barrier_semaphore(), self.groups - 1)
            self.tell(slice_sem, self.e, self.pair)

        @pl.when(self.core == 0)
        def _():
            pl.semaphore_wait(slice_sem, 1)


class Copies:
    def __init__(self, send, recv, local):
        self.sems = send, recv, local
        self.remote = self.near = 0
        self.pending = []

    def send(self, src, dst, to):
        send, recv, _ = self.sems
        copy = pltpu.make_async_remote_copy(
            src_ref=src,
            dst_ref=dst,
            send_sem=send.at[self.remote],
            recv_sem=recv.at[self.remote],
            device_id=to,
            device_id_type=MESH,
        )
        self.remote += 1
        copy.start()
        self.pending.append(copy)
        return copy

    def drain(self, copies):
        ids = {id(copy) for copy in copies}
        for copy in self.pending:
            if id(copy) in ids:
                copy.wait_send()
        self.pending = [copy for copy in self.pending if id(copy) not in ids]

    def keep(self, src, dst):
        copy = pltpu.make_async_copy(src, dst, self.sems[2].at[self.near])
        self.near += 1
        copy.start()
        return copy


GATE, UP, DOWN = range(3)
REMOTE = 128
LOCAL = 16


def chunks(ff):
    lanes = 128
    first = (ff // lanes + 1) // 2 * lanes
    return [pl.ds(0, first), pl.ds(first, ff - first)]


def route(groups, ids, gates):
    tok = ids.shape[1]
    rows = groups * MOST
    per_index = EXPERTS // groups
    slot = lax.broadcasted_iota(jnp.int32, (rows, tok), 0)
    target, place_in = jnp.zeros_like(slot), slot
    for g in range(1, groups):
        later = slot >= g * MOST
        target = target + jnp.where(later, per_index, 0)
        place_in = place_in - jnp.where(later, MOST, 0)
    chosen, gate_of = None, None
    vals = gates[...].astype(F32)
    for k in range(ids.shape[0]):
        hit = ids[pl.ds(k, 1), :] == target
        val = jnp.where(hit, vals[k : k + 1, :], 0.0)
        one = jnp.where(hit, 1.0, 0.0)
        chosen = one if chosen is None else chosen + one
        gate_of = val if gate_of is None else gate_of + val
    earlier = lax.broadcasted_iota(jnp.int32, (tok, tok), 0) < lax.broadcasted_iota(
        jnp.int32, (tok, tok), 1
    )
    rank = dot(chosen.astype(BF16), jnp.where(earlier, 1.0, 0.0).astype(BF16), ((1,), (0,)))
    place = (chosen > 0.0) & (rank == place_in.astype(F32))
    return (
        target,
        jnp.where(place, 1.0, 0.0).astype(BF16),
        jnp.where(place, gate_of, 0.0).astype(BF16),
    )


def layer_kernel(groups, *refs):
    ws, arrays_in = refs[:3], refs[3:7]
    owns, output, grad_tokens, grad_gates = refs[7:10], refs[10], refs[11], refs[12]
    full, xs, rows_in, acc, pre_out, pre_in, act = refs[13:20]
    pair_out, pair_in, near_in, back_in = refs[20:24]
    ids, gates, tokens, cotangent, pick, weighted = arrays = refs[24:30]
    at, go = Place(groups), Copies(*refs[30:33])
    block, ff = ws[0].shape
    rows = groups * MOST
    half_d = 4 * block
    cuts = chunks(ff)
    pair = (at.e, at.pair)
    across = [(at.e, at.to_y), (at.e, at.to_y), (at.e, at.to_x)]
    beside = [(at.e, at.to_x), (at.e, at.to_x), (at.e, at.to_y)]
    spot = [at.y, at.y, at.x]
    shape = (groups, MOST)
    first = ((0,), (0,))
    plain, turned = ((1,), (0,)), ((1,), (1,))
    top, low = pl.ds(0, rows), pl.ds(rows, rows)

    def span(q, s):
        return pl.ds(pl.multiple_of((2 * q + s) * block, block), block)

    def chip_span(q):
        return pl.ds(pl.multiple_of(2 * q * block, 2 * block), 2 * block)

    def fetch(m, c):
        return go.send(ws[m].at[:, c], full.at[m, span(spot[m], at.core), c], across[m])

    def near(m, c):
        where = full.at[m, span(spot[m], at.core), c]
        return [go.send(ws[m].at[:, c], where, pair), go.keep(ws[m].at[:, c], where)]

    def forward(m, c, copy):
        copy.wait_recv()
        where = full.at[m, span(1 - spot[m], at.core), c]
        return go.send(where, where, pair)

    def spread(src, dst, other, half):
        copies = []
        for step, there in at.planes():
            if half == 0 and step == 0:
                copies.append(go.keep(src.at[0, at.e], dst.at[0, at.e]))
            else:
                to = (there, other if half else at.f)
                copies.append(go.send(src.at[half, there], dst.at[half, at.e], to))
        return copies

    def wait_in(copies):
        for copy in copies:
            if copy.is_remote:
                copy.wait_recv()
            else:
                copy.wait()

    def x_cols(half, k):
        x = 1 - at.x if half else at.x
        return pl.ds(pl.multiple_of((4 * k + 2 * x) * block, 2 * block), 2 * block)

    def y_cols(half):
        y = 1 - at.y if half else at.y
        return pl.ds(pl.multiple_of(4 * y * block, half_d), half_d)

    loads = [go.keep(src, dst) for src, dst in zip(arrays_in, arrays)]
    plane_sem, slice_sem = refs[33:35]
    at.enter_plane(plane_sem)
    coming = {}
    nearby = {}
    for m in (GATE, UP):
        coming[m, 0] = fetch(m, cuts[0])
    coming[DOWN, 0] = fetch(DOWN, cuts[0])
    for m in (GATE, UP):
        nearby[m, 0] = near(m, cuts[0])
    wait_in(loads[:2])
    target, pick_val, weighted_val = route(groups, ids, gates)
    pick[...] = pick_val
    weighted[...] = weighted_val
    loads[2].wait()
    x_rows, og_rows = [], []
    for half in (1, 0):
        for k in range(2):
            val = dot(pick[...], tokens[:, x_cols(half, k)], plain).astype(BF16)
            xs[0, half, :, :, pl.ds(2 * k * block, 2 * block)] = val.reshape(shape + (2 * block,))
    at.enter_slice(slice_sem)
    for half in (1, 0):
        x_rows += spread(xs.at[0], rows_in.at[0], at.to_x, half)
    loads[3].wait()
    for half in (1, 0):
        val = dot(weighted[...], cotangent[:, y_cols(half)], plain).astype(BF16)
        xs[1, half] = val.reshape(shape + (half_d,))
    far = {(GATE, 0): forward(GATE, cuts[0], coming[GATE, 0])}
    coming[DOWN, 1] = fetch(DOWN, cuts[1])
    for half in (1, 0):
        og_rows += spread(xs.at[1], rows_in.at[1], at.to_y, half)
    for m in (GATE, UP):
        coming[m, 1] = fetch(m, cuts[1])
    for m, c in ((DOWN, 0), (DOWN, 1), (GATE, 1), (UP, 1)):
        nearby[m, c] = near(m, cuts[c])

    def lhs(t, cols):
        return rows_in[t, :, :, :, cols].reshape(2 * rows, -1)

    def begin(m, t, c):
        wait_in(nearby[m, c])
        cut, where = cuts[c], chip_span(spot[m])
        acc[m, :, cut] = dot(lhs(t, where), full[m, where, cut], plain)

    def finish(m, t, c, far):
        far.wait_recv()
        cut, where = cuts[c], chip_span(1 - spot[m])
        acc[m, :, cut] += dot(lhs(t, where), full[m, where, cut], plain)
        pre_out[m, top, cut] = acc[m, low, cut].astype(BF16)
        return go.send(pre_out.at[m, top, cut], pre_in.at[m, :, cut], beside[m])

    tile = 16

    def make_hidden(c):
        cut = cuts[c]

        def body(i, _):
            r = pl.ds(pl.multiple_of(i * tile, tile), tile)
            g = acc[GATE, r, cut] + pre_in[GATE, r, cut].astype(F32)
            u = acc[UP, r, cut] + pre_in[UP, r, cut].astype(F32)
            acc[GATE, r, cut] = g
            acc[UP, r, cut] = u
            act[DOWN, r, cut] = (g * jax.nn.sigmoid(g) * u).astype(BF16)
            return 0

        lax.fori_loop(0, rows // tile, body, 0)

    def make_grads(c):
        cut = cuts[c]

        def body(i, _):
            r = pl.ds(pl.multiple_of(i * tile, tile), tile)
            g, u = acc[GATE, r, cut], acc[UP, r, cut]
            h = acc[DOWN, r, cut] + pre_in[DOWN, r, cut].astype(F32)
            s = jax.nn.sigmoid(g)
            act[GATE, r, cut] = (h * u * s * (1.0 + g * (1.0 - s))).astype(BF16)
            act[UP, r, cut] = (h * g * s).astype(BF16)
            return 0

        lax.fori_loop(0, rows // tile, body, 0)

    def share(m, c):
        return go.send(act.at[m, top, cuts[c]], act.at[m, low, cuts[c]], beside[m])

    ends = []
    back_out = xs

    def grads(m, t, c):
        cut, q, other = cuts[c], spot[m], 1 - spot[m]

        def term(q, s):
            return dot(lhs(t, span(q, s)), act[m, :, cut], first)

        pair_out[m, 0, :, cut] = term(other, 1 - at.core).astype(BF16)
        to_far = go.send(pair_out.at[m, 0, :, cut], pair_in.at[m, 0, :, cut], pair)
        acc[m, pl.ds(0, block), cut] = term(other, at.core)
        pair_out[m, 1, :, cut] = term(q, 1 - at.core).astype(BF16)
        to_pair = go.send(pair_out.at[m, 1, :, cut], pair_in.at[m, 1, :, cut], pair)
        to_far.wait_recv()
        both = acc[m, pl.ds(0, block), cut] + pair_in[m, 0, :, cut].astype(F32)
        pre_out[m, :, cut] = both.astype(BF16)
        to_other = go.send(pre_out.at[m, :, cut], near_in.at[m, :, cut], across[m])
        owns[m][:, cut] = term(q, at.core)
        ends.append((m, c, to_other, to_pair))

    back, back_grad = [], []

    def send_out(half):
        r = low if half else top
        val = dot(act[DOWN, r], full[DOWN], turned)
        back_out[0, half] = val.astype(BF16).reshape(shape + (half_d,))
        back.extend(spread(back_out.at[0], back_in.at[0], at.to_y, half))

    def send_grad(half):
        r = low if half else top
        val = dot(act[GATE, r], full[GATE], turned) + dot(act[UP, r], full[UP], turned)
        back_out[1, half] = val.astype(BF16).reshape(shape + (half_d,))
        back_grad.extend(spread(back_out.at[1], back_in.at[1], at.to_x, half))

    pre, got = {}, {}
    far[UP, 0] = forward(UP, cuts[0], coming[UP, 0])
    wait_in(x_rows)
    for m in (GATE, UP):
        begin(m, 0, 0)
    for m in (GATE, UP):
        pre[m, 0] = finish(m, 0, 0, far[m, 0])
    for c in range(2):
        far[DOWN, c] = forward(DOWN, cuts[c], coming[DOWN, c])
    for m in (GATE, UP):
        begin(m, 0, 1)
    far[GATE, 1] = forward(GATE, cuts[1], coming[GATE, 1])
    wait_in(og_rows)
    for c in range(2):
        begin(DOWN, 1, c)
        pre[DOWN, c] = finish(DOWN, 1, c, far[DOWN, c])
    pre[GATE, 0].wait_recv()
    pre[UP, 0].wait_recv()
    make_hidden(0)
    got[DOWN, 0] = share(DOWN, 0)
    pre[GATE, 1] = finish(GATE, 0, 1, far[GATE, 1])
    far[UP, 1] = forward(UP, cuts[1], coming[UP, 1])
    pre[UP, 1] = finish(UP, 0, 1, far[UP, 1])
    pre[DOWN, 0].wait_recv()
    make_grads(0)
    for m in (GATE, UP):
        got[m, 0] = share(m, 0)
    pre[GATE, 1].wait_recv()
    pre[UP, 1].wait_recv()
    make_hidden(1)
    got[DOWN, 1] = share(DOWN, 1)
    go.drain(x_rows + og_rows)
    send_out(0)
    pre[DOWN, 1].wait_recv()
    make_grads(1)
    for m in (GATE, UP):
        got[m, 1] = share(m, 1)
    send_grad(0)

    go.drain(list(pre.values()))
    got[GATE, 0].wait_recv()
    grads(GATE, 0, 0)
    got[DOWN, 0].wait_recv()
    got[DOWN, 1].wait_recv()
    send_out(1)
    got[UP, 0].wait_recv()
    grads(UP, 0, 0)
    grads(DOWN, 1, 0)
    got[GATE, 1].wait_recv()
    got[UP, 1].wait_recv()
    send_grad(1)
    grads(GATE, 0, 1)
    grads(UP, 0, 1)
    grads(DOWN, 1, 1)

    wait_in(back)
    met = None
    for half in range(2):
        slot = back_in[0, half].reshape(rows, half_d)
        output[:, y_cols(half)] = dot(weighted[...], slot, first).astype(BF16)
        val = dot(slot, cotangent[:, y_cols(half)], turned)
        met = val if met is None else met + val
    met = jnp.where(pick[...].astype(F32) > 0.0, met, 0.0)
    for k in range(ids.shape[0]):
        hit = jnp.where(ids[pl.ds(k, 1), :] == target, met, 0.0)
        grad_gates[pl.ds(k, 1), :] = jnp.sum(hit, axis=0, keepdims=True)
    wait_in(back_grad)
    for half in range(2):
        for k in range(2):
            slot = back_in[1, half, :, :, pl.ds(2 * k * block, 2 * block)].reshape(rows, 2 * block)
            grad_tokens[:, x_cols(half, k)] = dot(pick[...], slot, first).astype(BF16)
    for m, c, to_other, to_pair in ends:
        cut = cuts[c]
        to_pair.wait_recv()
        to_other.wait_recv()
        owns[m][:, cut] += pair_in[m, 1, :, cut].astype(F32) + near_in[m, :, cut].astype(F32)
    go.drain(go.pending)


def stay(x):
    return pltpu.with_memory_space_constraint(x, pltpu.MemorySpace.HBM)


def layer_call(groups, ws, ids, gates, tokens, cotangent):
    dma = pltpu.SemaphoreType.DMA
    block, ff = ws[0].shape
    tok, width = tokens.shape
    rows = groups * MOST
    wide = (2, 2, groups, MOST, width // 2)
    vmem = pltpu.VMEM
    return pl.pallas_call(
        functools.partial(layer_kernel, groups),
        out_shape=[jax.ShapeDtypeStruct((block, ff), F32)] * 3
        + [jax.ShapeDtypeStruct((tok, width), BF16)] * 2
        + [jax.ShapeDtypeStruct(ids.shape, F32)],
        in_specs=[HBM] * 7,
        out_specs=[VMEM] * 6,
        scratch_shapes=[
            vmem((3, 4 * block, ff), BF16),
            vmem(wide, BF16),
            vmem(wide, BF16),
            vmem((3, 2 * rows, ff), F32),
            vmem((3, block, ff), BF16),
            vmem((3, rows, ff), BF16),
            vmem((3, 2 * rows, ff), BF16),
            vmem((3, 2, block, ff), BF16),
            vmem((3, 2, block, ff), BF16),
            vmem((3, block, ff), BF16),
            vmem(wide, BF16),
            vmem(ids.shape, ids.dtype),
            vmem(gates.shape, gates.dtype),
            vmem((tok, width), BF16),
            vmem((tok, width), BF16),
            vmem((rows, tok), BF16),
            vmem((rows, tok), BF16),
            dma((REMOTE,)),
            dma((REMOTE,)),
            dma((LOCAL,)),
            pltpu.SemaphoreType.REGULAR,
            pltpu.SemaphoreType.REGULAR,
        ],
        compiler_params=pltpu.CompilerParams(
            collective_id=0, has_side_effects=True, vmem_limit_bytes=41 * 2**20
        ),
    )(*map(stay, [*ws, ids, gates, tokens, cotangent]))


def store_kernel(*refs):
    n = len(refs) // 2
    srcs, dsts, sems = refs[:n], refs[n : 2 * n], refs[2 * n]
    copies = [pltpu.make_async_copy(srcs[i], dsts[i], sems.at[i]) for i in range(n)]
    for copy in copies:
        copy.start()
    for copy in copies:
        copy.wait()


def store_call(arrays):
    return pl.pallas_call(
        store_kernel,
        out_shape=[jax.ShapeDtypeStruct(a.shape, a.dtype) for a in arrays],
        in_specs=[VMEM] * len(arrays),
        out_specs=[HBM] * len(arrays),
        scratch_shapes=[pltpu.SemaphoreType.DMA((len(arrays),))],
        compiler_params=pltpu.CompilerParams(vmem_limit_bytes=2**20),
    )(*arrays)


def routes(expert_ids, gate_vals, groups):
    per_index = EXPERTS // groups
    window = WAVE * groups
    tok_count = expert_ids.shape[0]
    local_index = expert_ids % per_index
    window_slot = jnp.where(
        local_index < WAVE, expert_ids // per_index * WAVE + local_index, window
    )
    slot_is = window_slot[:, :, None] == jnp.arange(window, dtype=jnp.int32)[None, None, :]
    chosen = jnp.any(slot_is, axis=1)
    gate_of = jnp.sum(jnp.where(slot_is, gate_vals.astype(F32)[:, :, None], 0.0), axis=1)
    tok = jnp.arange(tok_count, dtype=jnp.int32)
    before = (tok[:, None] > tok[None, :]).astype(BF16)
    rank = dot(before, chosen.astype(BF16), ((1,), (0,))).astype(jnp.int32)
    place = chosen[:, :, None] & (
        rank[:, :, None] == jnp.arange(MOST, dtype=jnp.int32)[None, None, :]
    )
    pick = place.astype(BF16).reshape(tok_count, window * MOST)
    weighted = (
        jnp.where(place, gate_of[:, :, None], 0.0).astype(BF16).reshape(tok_count, window * MOST)
    )
    return slot_is, place, pick, weighted


def on_device(tokens, expert_ids, gate_vals, w_gate, w_up, w_down, cotangent):
    groups = lax.axis_size("expert")
    columns = lax.axis_size("fsdp")
    side = lax.axis_index("fsdp") % 2
    tok_count, width = tokens.shape
    block = w_gate.shape[1]
    rows = groups * MOST
    sides = [[i for i in range(columns) if i % 2 == s] for s in (0, 1)]
    pairs = [(i, i ^ 1) for i in range(columns)]

    def swap(x):
        return lax.ppermute(x, "fsdp", pairs)

    def gather(w):
        return lax.all_gather(w[0], "fsdp", axis_index_groups=sides, axis=0, tiled=True)

    def scatter(x):
        return lax.psum_scatter(
            x.astype(BF16), "fsdp", scatter_dimension=0, axis_index_groups=sides, tiled=True
        ).astype(F32)[None]

    def cut(x, odd):
        return jnp.concatenate(
            [x[:, (2 * k + odd) * block : (2 * k + odd + 1) * block] for k in range(columns // 2)],
            axis=1,
        )

    def halves(x):
        even, odd = cut(x, 0), cut(x, 1)
        return jnp.where(side == 0, even, odd), jnp.where(side == 0, odd, even)

    def whole_rows(mine, other):
        even, odd = jnp.where(side == 0, mine, other), jnp.where(side == 0, other, mine)
        parts = []
        for k in range(columns // 2):
            here = slice(k * block, (k + 1) * block)
            parts += [even[:, here], odd[:, here]]
        return jnp.concatenate(parts, axis=1)

    def exchange(mine, other):
        packed = jnp.stack(
            [mine.reshape(groups, MOST, width // 2), other.reshape(groups, MOST, width // 2)],
            axis=1,
        )
        there = lax.all_to_all(packed, "expert", split_axis=0, concat_axis=0, tiled=True)
        return there[:, 0].reshape(rows, width // 2), there[:, 1].reshape(rows, width // 2)

    square = columns == 8 and groups == 4
    first = ((0,), (0,))
    if square:
        results = layer_call(
            groups, [w_gate[0], w_up[0], w_down[0]], expert_ids.T, gate_vals.T, tokens, cotangent
        )
        *grad_w, output, grad_tokens, grad_gates = store_call(results)
        return (output, grad_tokens, grad_gates.T, *(g[None] for g in grad_w))
    slot_is, place, pick, weighted = routes(expert_ids, gate_vals, groups)
    full_gate, full_up, full_down = gather(w_gate), gather(w_up), gather(w_down)
    row_mine, row_other = exchange(*halves(dot(pick, tokens, first).astype(BF16)))
    og_mine, og_other = exchange(*halves(dot(weighted, cotangent, first).astype(BF16)))
    row_in = jnp.concatenate([row_mine, swap(row_other)], axis=0)
    out_grad = jnp.concatenate([og_mine, swap(og_other)], axis=0)

    def summed(x):
        return x[:rows] + swap(x[rows:].astype(BF16)).astype(F32)

    def both(x):
        return jnp.concatenate([x, swap(x)], axis=0)

    plain, turned = ((1,), (0,)), ((1,), (1,))
    gate_pre = summed(dot(row_in, full_gate, plain))
    up_pre = summed(dot(row_in, full_up, plain))
    sigmoid_g = jax.nn.sigmoid(gate_pre)
    hidden = (gate_pre * sigmoid_g * up_pre).astype(BF16)
    hidden_grad = summed(dot(out_grad, full_down, plain))
    gate_grad = (
        hidden_grad * up_pre * sigmoid_g * (1.0 + gate_pre * (1.0 - sigmoid_g))
    ).astype(BF16)
    up_grad = (hidden_grad * gate_pre * sigmoid_g).astype(BF16)
    hidden, gate_grad, up_grad = both(hidden), both(gate_grad), both(up_grad)
    grad_w_down = scatter(dot(out_grad, hidden, first))
    grad_w_gate = scatter(dot(row_in, gate_grad, first))
    grad_w_up = scatter(dot(row_in, up_grad, first))
    expert_out = dot(hidden, full_down, turned).astype(BF16)
    slot_grad = (dot(gate_grad, full_gate, turned) + dot(up_grad, full_up, turned)).astype(BF16)
    outs = exchange(expert_out[:rows], swap(expert_out[rows:]))
    grads = exchange(slot_grad[:rows], swap(slot_grad[rows:]))

    slot_out = whole_rows(*outs)
    output = dot(weighted, slot_out, plain).astype(BF16)
    grad_tokens = dot(pick, whole_rows(*grads), plain).astype(BF16)
    met = dot(cotangent, slot_out, turned)
    met = jnp.sum(jnp.where(place, met.reshape(place.shape), 0.0), axis=2)
    grad_gates = jnp.sum(jnp.where(slot_is, met[:, None, :], 0.0), axis=2)
    return (output, grad_tokens, grad_gates, grad_w_gate, grad_w_up, grad_w_down)


def solution(mesh):
    token = P(("expert", "fsdp"), None)
    weight = P("expert", "fsdp", None)
    return jax.shard_map(
        on_device,
        mesh=mesh,
        in_specs=(token, token, token, weight, weight, weight, token),
        out_specs=(token, token, token, weight, weight, weight),
        check_vma=False,
    )
```

```python
import functools

import jax
import jax.numpy as jnp
from jax import lax
from jax.experimental import pallas as pl
from jax.experimental.pallas import tpu as pltpu
from jax.sharding import PartitionSpec as P

EXPERTS = 64
WAVE = 1
MOST = 48
F32 = jnp.float32
BF16 = jnp.bfloat16


def dot(a, b, dims):
    return lax.dot_general(a, b, (dims, ((), ())), preferred_element_type=F32)


MESH = pl.DeviceIdType.MESH
HBM = pl.BlockSpec(memory_space=pltpu.MemorySpace.HBM)
VMEM = pl.BlockSpec(memory_space=pltpu.MemorySpace.VMEM)


class Place:
    def __init__(self, groups):
        self.groups = groups
        self.e = lax.axis_index("expert")
        f = lax.axis_index("fsdp")
        self.f = f
        self.core = f % 2
        self.x, self.y = (f // 2) % 2, f // 4
        self.pair = f + 1 - 2 * self.core
        self.others = [3 - self.e, (self.e + 2) % 4, self.e + 1 - 2 * (self.e % 2)]
        self.to_x, self.to_y = f + 2 - 4 * self.x, f + 4 - 8 * self.y

    def planes(self):
        return [(1, self.others[2]), (3, self.others[0]), (2, self.others[1]), (0, self.e)]

    def tell(self, sem, e, f):
        pl.semaphore_signal(sem, inc=1, device_id=(e, f), device_id_type=MESH)

    def enter_plane(self, plane_sem):
        sem = pltpu.get_barrier_semaphore()
        self.tell(sem, self.e, self.to_x - self.core)
        self.tell(sem, self.e, self.to_y - self.core)

        @pl.when(self.core == 1)
        def _():
            self.tell(sem, self.e, self.pair)

        @pl.when(self.core == 0)
        def _():
            pl.semaphore_wait(sem, 5)
            self.tell(plane_sem, self.e, self.pair)

        @pl.when(self.core == 1)
        def _():
            pl.semaphore_wait(plane_sem, 1)
            for there in self.others:
                self.tell(sem, there, self.f)

    def enter_slice(self, slice_sem):
        @pl.when(self.core == 1)
        def _():
            pl.semaphore_wait(pltpu.get_barrier_semaphore(), self.groups - 1)
            self.tell(slice_sem, self.e, self.pair)

        @pl.when(self.core == 0)
        def _():
            pl.semaphore_wait(slice_sem, 1)


class Copies:
    def __init__(self, send, recv, local):
        self.sems = send, recv, local
        self.remote = self.near = self.sending = 0
        self.free, self.slot = [], {}
        self.pending = []

    def send(self, src, dst, to):
        send, recv, _ = self.sems
        if self.free:
            slot = self.free.pop()
        else:
            slot, self.sending = self.sending, self.sending + 1
        copy = pltpu.make_async_remote_copy(
            src_ref=src,
            dst_ref=dst,
            send_sem=send.at[slot],
            recv_sem=recv.at[self.remote],
            device_id=to,
            device_id_type=MESH,
        )
        self.remote += 1
        copy.start()
        self.pending.append(copy)
        self.slot[id(copy)] = slot
        return copy

    def drain(self, copies):
        ids = {id(copy) for copy in copies}
        for copy in self.pending:
            if id(copy) in ids:
                copy.wait_send()
                self.free.append(self.slot[id(copy)])
        self.pending = [copy for copy in self.pending if id(copy) not in ids]

    def keep(self, src, dst):
        copy = pltpu.make_async_copy(src, dst, self.sems[2].at[self.near])
        self.near += 1
        copy.start()
        return copy


GATE, UP, DOWN = range(3)
SENDS = 56
REMOTE = 76
LOCAL = 14


def chunks(ff):
    lanes = 128
    first = (ff // lanes + 1) // 2 * lanes
    return [pl.ds(0, first), pl.ds(first, ff - first)]


def route(groups, ids, gates):
    tok = ids.shape[1]
    rows = groups * MOST
    per_index = EXPERTS // groups
    slot = lax.broadcasted_iota(jnp.int32, (rows, tok), 0)
    target, place_in = jnp.zeros_like(slot), slot
    for g in range(1, groups):
        later = slot >= g * MOST
        target = target + jnp.where(later, per_index, 0)
        place_in = place_in - jnp.where(later, MOST, 0)
    chosen, gate_of = None, None
    vals = gates[...].astype(F32)
    for k in range(ids.shape[0]):
        hit = ids[pl.ds(k, 1), :] == target
        val = jnp.where(hit, vals[k : k + 1, :], 0.0)
        one = jnp.where(hit, 1.0, 0.0)
        chosen = one if chosen is None else chosen + one
        gate_of = val if gate_of is None else gate_of + val
    earlier = lax.broadcasted_iota(jnp.int32, (tok, tok), 0) < lax.broadcasted_iota(
        jnp.int32, (tok, tok), 1
    )
    rank = dot(chosen.astype(BF16), jnp.where(earlier, 1.0, 0.0).astype(BF16), ((1,), (0,)))
    place = (chosen > 0.0) & (rank == place_in.astype(F32))
    return (
        target,
        jnp.where(place, 1.0, 0.0).astype(BF16),
        jnp.where(place, gate_of, 0.0).astype(BF16),
    )


def layer_kernel(groups, *refs):
    ws, arrays_in = refs[:3], refs[3:7]
    owns, output, grad_tokens, grad_gates = refs[7:10], refs[10], refs[11], refs[12]
    full, xs, rows_in, acc, pre_out, pre_in, act = refs[13:20]
    pair_out, pair_in, near_in, back_in = refs[20:24]
    ids, gates, tokens, cotangent, pick, weighted = arrays = refs[24:30]
    at, go = Place(groups), Copies(*refs[30:33])
    block, ff = ws[0].shape
    rows = groups * MOST
    half_d = 4 * block
    cuts = chunks(ff)
    pair = (at.e, at.pair)
    across = [(at.e, at.to_y), (at.e, at.to_y), (at.e, at.to_x)]
    beside = [(at.e, at.to_x), (at.e, at.to_x), (at.e, at.to_y)]
    spot = [at.y, at.y, at.x]
    shape = (groups, MOST)
    first = ((0,), (0,))
    plain, turned = ((1,), (0,)), ((1,), (1,))
    top, low = pl.ds(0, rows), pl.ds(rows, rows)

    def span(q, s):
        return pl.ds(pl.multiple_of((2 * q + s) * block, block), block)

    def chip_span(q):
        return pl.ds(pl.multiple_of(2 * q * block, 2 * block), 2 * block)

    def fetch(m, c):
        return go.send(ws[m].at[:, c], full.at[m, span(spot[m], at.core), c], across[m])

    def near(m, c):
        where = full.at[m, span(spot[m], at.core), c]
        return [go.send(ws[m].at[:, c], where, pair), go.keep(ws[m].at[:, c], where)]

    def forward(m, c, copy):
        copy.wait_recv()
        where = full.at[m, span(1 - spot[m], at.core), c]
        return go.send(where, where, pair)

    def spread(src, dst, other, half):
        copies = []
        for step, there in at.planes():
            if half == 0 and step == 0:
                copies.append(go.keep(src.at[0, at.e], dst.at[0, at.e]))
            else:
                to = (there, other if half else at.f)
                copies.append(go.send(src.at[half, there], dst.at[half, at.e], to))
        return copies

    def wait_in(copies):
        for copy in copies:
            if copy.is_remote:
                copy.wait_recv()
            else:
                copy.wait()

    def x_cols(half, k):
        x = 1 - at.x if half else at.x
        return pl.ds(pl.multiple_of((4 * k + 2 * x) * block, 2 * block), 2 * block)

    def y_cols(half):
        y = 1 - at.y if half else at.y
        return pl.ds(pl.multiple_of(4 * y * block, half_d), half_d)

    loads = [go.keep(src, dst) for src, dst in zip(arrays_in, arrays)]
    plane_sem, slice_sem = refs[33:35]
    at.enter_plane(plane_sem)
    coming = {}
    nearby = {}
    for m in (GATE, UP):
        coming[m, 0] = fetch(m, cuts[0])
    coming[DOWN, 0] = fetch(DOWN, cuts[0])
    for m in (GATE, UP):
        nearby[m, 0] = near(m, cuts[0])
    wait_in(loads[:2])
    target, pick_val, weighted_val = route(groups, ids, gates)
    pick[...] = pick_val
    weighted[...] = weighted_val
    loads[2].wait()
    x_rows, og_rows = [], []
    for half in (1, 0):
        for k in range(2):
            val = dot(pick[...], tokens[:, x_cols(half, k)], plain).astype(BF16)
            xs[0, half, :, :, pl.ds(2 * k * block, 2 * block)] = val.reshape(shape + (2 * block,))
    at.enter_slice(slice_sem)
    for half in (1, 0):
        x_rows += spread(xs.at[0], rows_in.at[0], at.to_x, half)
    loads[3].wait()
    for half in (1, 0):
        val = dot(weighted[...], cotangent[:, y_cols(half)], plain).astype(BF16)
        xs[1, half] = val.reshape(shape + (half_d,))
    far = {(GATE, 0): forward(GATE, cuts[0], coming[GATE, 0])}
    coming[DOWN, 1] = fetch(DOWN, cuts[1])
    for half in (1, 0):
        og_rows += spread(xs.at[1], rows_in.at[1], at.to_y, half)
    for m in (GATE, UP):
        coming[m, 1] = fetch(m, cuts[1])
    for m, c in ((DOWN, 0), (DOWN, 1), (GATE, 1), (UP, 1)):
        nearby[m, c] = near(m, cuts[c])

    def lhs(t, cols):
        return rows_in[t, :, :, :, cols].reshape(2 * rows, -1)

    def begin(m, t, c):
        wait_in(nearby[m, c])
        cut, where = cuts[c], chip_span(spot[m])
        acc[m, :, cut] = dot(lhs(t, where), full[m, where, cut], plain)

    def finish(m, t, c, far):
        far.wait_recv()
        cut, where = cuts[c], chip_span(1 - spot[m])
        acc[m, :, cut] += dot(lhs(t, where), full[m, where, cut], plain)
        pre_out[m, top, cut] = acc[m, low, cut].astype(BF16)
        return go.send(pre_out.at[m, top, cut], pre_in.at[m, :, cut], beside[m])

    tile = 16

    def make_hidden(c):
        cut = cuts[c]

        def body(i, _):
            r = pl.ds(pl.multiple_of(i * tile, tile), tile)
            g = acc[GATE, r, cut] + pre_in[GATE, r, cut].astype(F32)
            u = acc[UP, r, cut] + pre_in[UP, r, cut].astype(F32)
            acc[GATE, r, cut] = g
            acc[UP, r, cut] = u
            act[DOWN, r, cut] = (g * jax.nn.sigmoid(g) * u).astype(BF16)
            return 0

        lax.fori_loop(0, rows // tile, body, 0)

    def make_grads(c):
        cut = cuts[c]

        def body(i, _):
            r = pl.ds(pl.multiple_of(i * tile, tile), tile)
            g, u = acc[GATE, r, cut], acc[UP, r, cut]
            h = acc[DOWN, r, cut] + pre_in[DOWN, r, cut].astype(F32)
            s = jax.nn.sigmoid(g)
            act[GATE, r, cut] = (h * u * s * (1.0 + g * (1.0 - s))).astype(BF16)
            act[UP, r, cut] = (h * g * s).astype(BF16)
            return 0

        lax.fori_loop(0, rows // tile, body, 0)

    def share(m, c):
        return go.send(act.at[m, top, cuts[c]], act.at[m, low, cuts[c]], beside[m])

    ends = []
    back_out = xs

    def grads(m, t, c):
        cut, q, other = cuts[c], spot[m], 1 - spot[m]

        def term(q, s):
            return dot(lhs(t, span(q, s)), act[m, :, cut], first)

        pair_out[m, 0, :, cut] = term(other, 1 - at.core).astype(BF16)
        to_far = go.send(pair_out.at[m, 0, :, cut], pair_in.at[m, 0, :, cut], pair)
        acc[m, pl.ds(0, block), cut] = term(other, at.core)
        pair_out[m, 1, :, cut] = term(q, 1 - at.core).astype(BF16)
        to_pair = go.send(pair_out.at[m, 1, :, cut], pair_in.at[m, 1, :, cut], pair)
        to_far.wait_recv()
        both = acc[m, pl.ds(0, block), cut] + pair_in[m, 0, :, cut].astype(F32)
        pre_out[m, :, cut] = both.astype(BF16)
        to_other = go.send(pre_out.at[m, :, cut], near_in.at[m, :, cut], across[m])
        owns[m][:, cut] = term(q, at.core)
        ends.append((m, c, to_other, to_pair))

    back, back_grad = [], []

    def send_out(half):
        r = low if half else top
        val = dot(act[DOWN, r], full[DOWN], turned)
        back_out[0, half] = val.astype(BF16).reshape(shape + (half_d,))
        back.extend(spread(back_out.at[0], back_in.at[0], at.to_y, half))

    def send_grad(half):
        r = low if half else top
        val = dot(act[GATE, r], full[GATE], turned) + dot(act[UP, r], full[UP], turned)
        back_out[1, half] = val.astype(BF16).reshape(shape + (half_d,))
        back_grad.extend(spread(back_out.at[1], back_in.at[1], at.to_x, half))

    pre, got = {}, {}
    far[UP, 0] = forward(UP, cuts[0], coming[UP, 0])
    wait_in(x_rows)
    for m in (GATE, UP):
        begin(m, 0, 0)
    for m in (GATE, UP):
        pre[m, 0] = finish(m, 0, 0, far[m, 0])
    for c in range(2):
        far[DOWN, c] = forward(DOWN, cuts[c], coming[DOWN, c])
    for m in (GATE, UP):
        begin(m, 0, 1)
    far[GATE, 1] = forward(GATE, cuts[1], coming[GATE, 1])
    wait_in(og_rows)
    for c in range(2):
        begin(DOWN, 1, c)
        pre[DOWN, c] = finish(DOWN, 1, c, far[DOWN, c])
    pre[GATE, 0].wait_recv()
    pre[UP, 0].wait_recv()
    make_hidden(0)
    got[DOWN, 0] = share(DOWN, 0)
    pre[GATE, 1] = finish(GATE, 0, 1, far[GATE, 1])
    far[UP, 1] = forward(UP, cuts[1], coming[UP, 1])
    pre[UP, 1] = finish(UP, 0, 1, far[UP, 1])
    pre[DOWN, 0].wait_recv()
    make_grads(0)
    for m in (GATE, UP):
        got[m, 0] = share(m, 0)
    pre[GATE, 1].wait_recv()
    pre[UP, 1].wait_recv()
    make_hidden(1)
    got[DOWN, 1] = share(DOWN, 1)
    go.drain(x_rows + og_rows)
    send_out(0)
    pre[DOWN, 1].wait_recv()
    make_grads(1)
    for m in (GATE, UP):
        got[m, 1] = share(m, 1)
    send_grad(0)

    go.drain(list(pre.values()))
    got[GATE, 0].wait_recv()
    grads(GATE, 0, 0)
    got[DOWN, 0].wait_recv()
    got[DOWN, 1].wait_recv()
    send_out(1)
    got[UP, 0].wait_recv()
    grads(UP, 0, 0)
    grads(DOWN, 1, 0)
    got[GATE, 1].wait_recv()
    got[UP, 1].wait_recv()
    send_grad(1)
    grads(GATE, 0, 1)
    grads(UP, 0, 1)
    grads(DOWN, 1, 1)

    wait_in(back)
    met = None
    for half in range(2):
        slot = back_in[0, half].reshape(rows, half_d)
        output[:, y_cols(half)] = dot(weighted[...], slot, first).astype(BF16)
        val = dot(slot, cotangent[:, y_cols(half)], turned)
        met = val if met is None else met + val
    met = jnp.where(pick[...].astype(F32) > 0.0, met, 0.0)
    for k in range(ids.shape[0]):
        hit = jnp.where(ids[pl.ds(k, 1), :] == target, met, 0.0)
        grad_gates[pl.ds(k, 1), :] = jnp.sum(hit, axis=0, keepdims=True)
    wait_in(back_grad)
    for half in range(2):
        for k in range(2):
            slot = back_in[1, half, :, :, pl.ds(2 * k * block, 2 * block)].reshape(rows, 2 * block)
            grad_tokens[:, x_cols(half, k)] = dot(pick[...], slot, first).astype(BF16)
    for m, c, to_other, to_pair in ends:
        cut = cuts[c]
        to_pair.wait_recv()
        to_other.wait_recv()
        owns[m][:, cut] += pair_in[m, 1, :, cut].astype(F32) + near_in[m, :, cut].astype(F32)
    go.drain(go.pending)
    assert (go.sending, go.remote, go.near) == (SENDS, REMOTE, LOCAL)


def stay(x):
    return pltpu.with_memory_space_constraint(x, pltpu.MemorySpace.HBM)


def layer_call(groups, ws, ids, gates, tokens, cotangent):
    dma = pltpu.SemaphoreType.DMA
    block, ff = ws[0].shape
    tok, width = tokens.shape
    rows = groups * MOST
    wide = (2, 2, groups, MOST, width // 2)
    vmem = pltpu.VMEM
    return pl.pallas_call(
        functools.partial(layer_kernel, groups),
        out_shape=[jax.ShapeDtypeStruct((block, ff), F32)] * 3
        + [jax.ShapeDtypeStruct((tok, width), BF16)] * 2
        + [jax.ShapeDtypeStruct(ids.shape, F32)],
        in_specs=[HBM] * 7,
        out_specs=[VMEM] * 6,
        scratch_shapes=[
            vmem((3, 4 * block, ff), BF16),
            vmem(wide, BF16),
            vmem(wide, BF16),
            vmem((3, 2 * rows, ff), F32),
            vmem((3, block, ff), BF16),
            vmem((3, rows, ff), BF16),
            vmem((3, 2 * rows, ff), BF16),
            vmem((3, 2, block, ff), BF16),
            vmem((3, 2, block, ff), BF16),
            vmem((3, block, ff), BF16),
            vmem(wide, BF16),
            vmem(ids.shape, ids.dtype),
            vmem(gates.shape, gates.dtype),
            vmem((tok, width), BF16),
            vmem((tok, width), BF16),
            vmem((rows, tok), BF16),
            vmem((rows, tok), BF16),
            dma((SENDS,)),
            dma((REMOTE,)),
            dma((LOCAL,)),
            pltpu.SemaphoreType.REGULAR,
            pltpu.SemaphoreType.REGULAR,
        ],
        compiler_params=pltpu.CompilerParams(
            collective_id=0, has_side_effects=True, vmem_limit_bytes=41 * 2**20
        ),
    )(*map(stay, [*ws, ids, gates, tokens, cotangent]))


def store_kernel(*refs):
    n = len(refs) // 2
    srcs, dsts, sems = refs[:n], refs[n : 2 * n], refs[2 * n]
    copies = [pltpu.make_async_copy(srcs[i], dsts[i], sems.at[i]) for i in range(n)]
    for copy in copies:
        copy.start()
    for copy in copies:
        copy.wait()


def store_call(arrays):
    return pl.pallas_call(
        store_kernel,
        out_shape=[jax.ShapeDtypeStruct(a.shape, a.dtype) for a in arrays],
        in_specs=[VMEM] * len(arrays),
        out_specs=[HBM] * len(arrays),
        scratch_shapes=[pltpu.SemaphoreType.DMA((len(arrays),))],
        compiler_params=pltpu.CompilerParams(vmem_limit_bytes=2**20),
    )(*arrays)


def routes(expert_ids, gate_vals, groups):
    per_index = EXPERTS // groups
    window = WAVE * groups
    tok_count = expert_ids.shape[0]
    local_index = expert_ids % per_index
    window_slot = jnp.where(
        local_index < WAVE, expert_ids // per_index * WAVE + local_index, window
    )
    slot_is = window_slot[:, :, None] == jnp.arange(window, dtype=jnp.int32)[None, None, :]
    chosen = jnp.any(slot_is, axis=1)
    gate_of = jnp.sum(jnp.where(slot_is, gate_vals.astype(F32)[:, :, None], 0.0), axis=1)
    tok = jnp.arange(tok_count, dtype=jnp.int32)
    before = (tok[:, None] > tok[None, :]).astype(BF16)
    rank = dot(before, chosen.astype(BF16), ((1,), (0,))).astype(jnp.int32)
    place = chosen[:, :, None] & (
        rank[:, :, None] == jnp.arange(MOST, dtype=jnp.int32)[None, None, :]
    )
    pick = place.astype(BF16).reshape(tok_count, window * MOST)
    weighted = (
        jnp.where(place, gate_of[:, :, None], 0.0).astype(BF16).reshape(tok_count, window * MOST)
    )
    return slot_is, place, pick, weighted


def on_device(tokens, expert_ids, gate_vals, w_gate, w_up, w_down, cotangent):
    groups = lax.axis_size("expert")
    columns = lax.axis_size("fsdp")
    side = lax.axis_index("fsdp") % 2
    tok_count, width = tokens.shape
    block = w_gate.shape[1]
    rows = groups * MOST
    sides = [[i for i in range(columns) if i % 2 == s] for s in (0, 1)]
    pairs = [(i, i ^ 1) for i in range(columns)]

    def swap(x):
        return lax.ppermute(x, "fsdp", pairs)

    def gather(w):
        return lax.all_gather(w[0], "fsdp", axis_index_groups=sides, axis=0, tiled=True)

    def scatter(x):
        return lax.psum_scatter(
            x.astype(BF16), "fsdp", scatter_dimension=0, axis_index_groups=sides, tiled=True
        ).astype(F32)[None]

    def cut(x, odd):
        return jnp.concatenate(
            [x[:, (2 * k + odd) * block : (2 * k + odd + 1) * block] for k in range(columns // 2)],
            axis=1,
        )

    def halves(x):
        even, odd = cut(x, 0), cut(x, 1)
        return jnp.where(side == 0, even, odd), jnp.where(side == 0, odd, even)

    def whole_rows(mine, other):
        even, odd = jnp.where(side == 0, mine, other), jnp.where(side == 0, other, mine)
        parts = []
        for k in range(columns // 2):
            here = slice(k * block, (k + 1) * block)
            parts += [even[:, here], odd[:, here]]
        return jnp.concatenate(parts, axis=1)

    def exchange(mine, other):
        packed = jnp.stack(
            [mine.reshape(groups, MOST, width // 2), other.reshape(groups, MOST, width // 2)],
            axis=1,
        )
        there = lax.all_to_all(packed, "expert", split_axis=0, concat_axis=0, tiled=True)
        return there[:, 0].reshape(rows, width // 2), there[:, 1].reshape(rows, width // 2)

    square = columns == 8 and groups == 4
    first = ((0,), (0,))
    if square:
        results = layer_call(
            groups, [w_gate[0], w_up[0], w_down[0]], expert_ids.T, gate_vals.T, tokens, cotangent
        )
        *grad_w, output, grad_tokens, grad_gates = store_call(results)
        return (output, grad_tokens, grad_gates.T, *(g[None] for g in grad_w))
    slot_is, place, pick, weighted = routes(expert_ids, gate_vals, groups)
    full_gate, full_up, full_down = gather(w_gate), gather(w_up), gather(w_down)
    row_mine, row_other = exchange(*halves(dot(pick, tokens, first).astype(BF16)))
    og_mine, og_other = exchange(*halves(dot(weighted, cotangent, first).astype(BF16)))
    row_in = jnp.concatenate([row_mine, swap(row_other)], axis=0)
    out_grad = jnp.concatenate([og_mine, swap(og_other)], axis=0)

    def summed(x):
        return x[:rows] + swap(x[rows:].astype(BF16)).astype(F32)

    def both(x):
        return jnp.concatenate([x, swap(x)], axis=0)

    plain, turned = ((1,), (0,)), ((1,), (1,))
    gate_pre = summed(dot(row_in, full_gate, plain))
    up_pre = summed(dot(row_in, full_up, plain))
    sigmoid_g = jax.nn.sigmoid(gate_pre)
    hidden = (gate_pre * sigmoid_g * up_pre).astype(BF16)
    hidden_grad = summed(dot(out_grad, full_down, plain))
    gate_grad = (
        hidden_grad * up_pre * sigmoid_g * (1.0 + gate_pre * (1.0 - sigmoid_g))
    ).astype(BF16)
    up_grad = (hidden_grad * gate_pre * sigmoid_g).astype(BF16)
    hidden, gate_grad, up_grad = both(hidden), both(gate_grad), both(up_grad)
    grad_w_down = scatter(dot(out_grad, hidden, first))
    grad_w_gate = scatter(dot(row_in, gate_grad, first))
    grad_w_up = scatter(dot(row_in, up_grad, first))
    expert_out = dot(hidden, full_down, turned).astype(BF16)
    slot_grad = (dot(gate_grad, full_gate, turned) + dot(up_grad, full_up, turned)).astype(BF16)
    outs = exchange(expert_out[:rows], swap(expert_out[rows:]))
    grads = exchange(slot_grad[:rows], swap(slot_grad[rows:]))

    slot_out = whole_rows(*outs)
    output = dot(weighted, slot_out, plain).astype(BF16)
    grad_tokens = dot(pick, whole_rows(*grads), plain).astype(BF16)
    met = dot(cotangent, slot_out, turned)
    met = jnp.sum(jnp.where(place, met.reshape(place.shape), 0.0), axis=2)
    grad_gates = jnp.sum(jnp.where(slot_is, met[:, None, :], 0.0), axis=2)
    return (output, grad_tokens, grad_gates, grad_w_gate, grad_w_up, grad_w_down)


def solution(mesh):
    token = P(("expert", "fsdp"), None)
    weight = P("expert", "fsdp", None)
    return jax.shard_map(
        on_device,
        mesh=mesh,
        in_specs=(token, token, token, weight, weight, weight, token),
        out_specs=(token, token, token, weight, weight, weight),
        check_vma=False,
    )
```

```python
import functools

import jax
import jax.numpy as jnp
from jax import lax
from jax.experimental import pallas as pl
from jax.experimental.pallas import tpu as pltpu
from jax.sharding import PartitionSpec as P

EXPERTS = 64
WAVE = 1
MOST = 48
F32 = jnp.float32
BF16 = jnp.bfloat16


def dot(a, b, dims):
    return lax.dot_general(a, b, (dims, ((), ())), preferred_element_type=F32)


MESH = pl.DeviceIdType.MESH
HBM = pl.BlockSpec(memory_space=pltpu.MemorySpace.HBM)
VMEM = pl.BlockSpec(memory_space=pltpu.MemorySpace.VMEM)


class Place:
    def __init__(self, groups):
        self.groups = groups
        self.e = lax.axis_index("expert")
        f = lax.axis_index("fsdp")
        self.f = f
        self.core = f % 2
        self.x, self.y = (f // 2) % 2, f // 4
        self.pair = f + 1 - 2 * self.core
        self.others = [3 - self.e, (self.e + 2) % 4, self.e + 1 - 2 * (self.e % 2)]
        self.to_x, self.to_y = f + 2 - 4 * self.x, f + 4 - 8 * self.y

    def planes(self):
        return [(1, self.others[2]), (3, self.others[0]), (2, self.others[1]), (0, self.e)]

    def tell(self, sem, e, f):
        pl.semaphore_signal(sem, inc=1, device_id=(e, f), device_id_type=MESH)

    def enter_plane(self, plane_sem):
        sem = pltpu.get_barrier_semaphore()
        self.tell(sem, self.e, self.to_x - self.core)
        self.tell(sem, self.e, self.to_y - self.core)

        @pl.when(self.core == 1)
        def _():
            self.tell(sem, self.e, self.pair)

        @pl.when(self.core == 0)
        def _():
            pl.semaphore_wait(sem, 5)
            self.tell(plane_sem, self.e, self.pair)

        @pl.when(self.core == 1)
        def _():
            pl.semaphore_wait(plane_sem, 1)
            for there in self.others:
                self.tell(sem, there, self.f)

    def enter_slice(self, slice_sem):
        @pl.when(self.core == 1)
        def _():
            pl.semaphore_wait(pltpu.get_barrier_semaphore(), self.groups - 1)
            self.tell(slice_sem, self.e, self.pair)

        @pl.when(self.core == 0)
        def _():
            pl.semaphore_wait(slice_sem, 1)


class Copies:
    def __init__(self, send, recv, local):
        self.sems = send, recv, local
        self.remote = self.near = self.sending = 0
        self.free, self.slot = [], {}
        self.pending = []

    def send(self, src, dst, to):
        send, recv, _ = self.sems
        if self.free:
            slot = self.free.pop()
        else:
            slot, self.sending = self.sending, self.sending + 1
        copy = pltpu.make_async_remote_copy(
            src_ref=src,
            dst_ref=dst,
            send_sem=send.at[slot],
            recv_sem=recv.at[self.remote],
            device_id=to,
            device_id_type=MESH,
        )
        self.remote += 1
        copy.start()
        self.pending.append(copy)
        self.slot[id(copy)] = slot
        return copy

    def drain(self, copies):
        ids = {id(copy) for copy in copies}
        for copy in self.pending:
            if id(copy) in ids:
                copy.wait_send()
                self.free.append(self.slot[id(copy)])
        self.pending = [copy for copy in self.pending if id(copy) not in ids]

    def keep(self, src, dst):
        copy = pltpu.make_async_copy(src, dst, self.sems[2].at[self.near])
        self.near += 1
        copy.start()
        return copy


GATE, UP, DOWN = range(3)
SENDS = 42
REMOTE = 76
LOCAL = 14


def chunks(ff):
    lanes = 128
    first = (ff // lanes + 1) // 2 * lanes
    return [pl.ds(0, first), pl.ds(first, ff - first)]


def route(groups, ids, gates):
    tok = ids.shape[1]
    rows = groups * MOST
    per_index = EXPERTS // groups
    slot = lax.broadcasted_iota(jnp.int32, (rows, tok), 0)
    target, place_in = jnp.zeros_like(slot), slot
    for g in range(1, groups):
        later = slot >= g * MOST
        target = target + jnp.where(later, per_index, 0)
        place_in = place_in - jnp.where(later, MOST, 0)
    chosen, gate_of = None, None
    vals = gates[...].astype(F32)
    for k in range(ids.shape[0]):
        hit = ids[pl.ds(k, 1), :] == target
        val = jnp.where(hit, vals[k : k + 1, :], 0.0)
        one = jnp.where(hit, 1.0, 0.0)
        chosen = one if chosen is None else chosen + one
        gate_of = val if gate_of is None else gate_of + val
    earlier = lax.broadcasted_iota(jnp.int32, (tok, tok), 0) < lax.broadcasted_iota(
        jnp.int32, (tok, tok), 1
    )
    rank = dot(chosen.astype(BF16), jnp.where(earlier, 1.0, 0.0).astype(BF16), ((1,), (0,)))
    place = (chosen > 0.0) & (rank == place_in.astype(F32))
    return (
        target,
        jnp.where(place, 1.0, 0.0).astype(BF16),
        jnp.where(place, gate_of, 0.0).astype(BF16),
    )


def layer_kernel(groups, *refs):
    ws, arrays_in = refs[:3], refs[3:7]
    owns, output, grad_tokens, grad_gates = refs[7:10], refs[10], refs[11], refs[12]
    full, xs, rows_in, acc, pre_out, pre_in, act = refs[13:20]
    pair_out, pair_in, near_in, back_in = refs[20:24]
    ids, gates, tokens, cotangent, pick, weighted = arrays = refs[24:30]
    at, go = Place(groups), Copies(*refs[30:33])
    block, ff = ws[0].shape
    rows = groups * MOST
    half_d = 4 * block
    cuts = chunks(ff)
    pair = (at.e, at.pair)
    across = [(at.e, at.to_y), (at.e, at.to_y), (at.e, at.to_x)]
    beside = [(at.e, at.to_x), (at.e, at.to_x), (at.e, at.to_y)]
    spot = [at.y, at.y, at.x]
    shape = (groups, MOST)
    first = ((0,), (0,))
    plain, turned = ((1,), (0,)), ((1,), (1,))
    top, low = pl.ds(0, rows), pl.ds(rows, rows)

    def span(q, s):
        return pl.ds(pl.multiple_of((2 * q + s) * block, block), block)

    def chip_span(q):
        return pl.ds(pl.multiple_of(2 * q * block, 2 * block), 2 * block)

    def fetch(m, c):
        return go.send(ws[m].at[:, c], full.at[m, span(spot[m], at.core), c], across[m])

    def near(m, c):
        where = full.at[m, span(spot[m], at.core), c]
        return [go.send(ws[m].at[:, c], where, pair), go.keep(ws[m].at[:, c], where)]

    def forward(m, c, copy):
        copy.wait_recv()
        where = full.at[m, span(1 - spot[m], at.core), c]
        return go.send(where, where, pair)

    def spread(src, dst, other, half):
        copies = []
        for step, there in at.planes():
            if half == 0 and step == 0:
                copies.append(go.keep(src.at[0, at.e], dst.at[0, at.e]))
            else:
                to = (there, other if half else at.f)
                copies.append(go.send(src.at[half, there], dst.at[half, at.e], to))
        return copies

    def wait_in(copies):
        for copy in copies:
            if copy.is_remote:
                copy.wait_recv()
            else:
                copy.wait()

    def x_cols(half, k):
        x = 1 - at.x if half else at.x
        return pl.ds(pl.multiple_of((4 * k + 2 * x) * block, 2 * block), 2 * block)

    def y_cols(half):
        y = 1 - at.y if half else at.y
        return pl.ds(pl.multiple_of(4 * y * block, half_d), half_d)

    loads = [go.keep(src, dst) for src, dst in zip(arrays_in, arrays)]
    plane_sem, slice_sem = refs[33:35]
    at.enter_plane(plane_sem)
    coming = {}
    nearby = {}
    for m in (GATE, UP):
        coming[m, 0] = fetch(m, cuts[0])
    coming[DOWN, 0] = fetch(DOWN, cuts[0])
    for m in (GATE, UP):
        nearby[m, 0] = near(m, cuts[0])
    wait_in(loads[:2])
    target, pick_val, weighted_val = route(groups, ids, gates)
    pick[...] = pick_val
    weighted[...] = weighted_val
    loads[2].wait()
    x_rows, og_rows = [], []
    for half in (1, 0):
        for k in range(2):
            val = dot(pick[...], tokens[:, x_cols(half, k)], plain).astype(BF16)
            xs[0, half, :, :, pl.ds(2 * k * block, 2 * block)] = val.reshape(shape + (2 * block,))
    at.enter_slice(slice_sem)
    for half in (1, 0):
        x_rows += spread(xs.at[0], rows_in.at[0], at.to_x, half)
    loads[3].wait()
    for half in (1, 0):
        val = dot(weighted[...], cotangent[:, y_cols(half)], plain).astype(BF16)
        xs[1, half] = val.reshape(shape + (half_d,))
    far = {(GATE, 0): forward(GATE, cuts[0], coming[GATE, 0])}
    coming[DOWN, 1] = fetch(DOWN, cuts[1])
    for half in (1, 0):
        og_rows += spread(xs.at[1], rows_in.at[1], at.to_y, half)
    for m in (GATE, UP):
        coming[m, 1] = fetch(m, cuts[1])
    for m, c in ((DOWN, 0), (DOWN, 1), (GATE, 1), (UP, 1)):
        nearby[m, c] = near(m, cuts[c])

    def lhs(t, cols):
        return rows_in[t, :, :, :, cols].reshape(2 * rows, -1)

    def begin(m, t, c):
        wait_in(nearby[m, c])
        cut, where = cuts[c], chip_span(spot[m])
        acc[m, :, cut] = dot(lhs(t, where), full[m, where, cut], plain)

    def finish(m, t, c, far):
        far.wait_recv()
        cut, where = cuts[c], chip_span(1 - spot[m])
        acc[m, :, cut] += dot(lhs(t, where), full[m, where, cut], plain)
        pre_out[m, top, cut] = acc[m, low, cut].astype(BF16)
        return go.send(pre_out.at[m, top, cut], pre_in.at[m, :, cut], beside[m])

    tile = 16

    def make_hidden(c):
        cut = cuts[c]

        def body(i, _):
            r = pl.ds(pl.multiple_of(i * tile, tile), tile)
            g = acc[GATE, r, cut] + pre_in[GATE, r, cut].astype(F32)
            u = acc[UP, r, cut] + pre_in[UP, r, cut].astype(F32)
            acc[GATE, r, cut] = g
            acc[UP, r, cut] = u
            act[DOWN, r, cut] = (g * jax.nn.sigmoid(g) * u).astype(BF16)
            return 0

        lax.fori_loop(0, rows // tile, body, 0)

    def make_grads(c):
        cut = cuts[c]

        def body(i, _):
            r = pl.ds(pl.multiple_of(i * tile, tile), tile)
            g, u = acc[GATE, r, cut], acc[UP, r, cut]
            h = acc[DOWN, r, cut] + pre_in[DOWN, r, cut].astype(F32)
            s = jax.nn.sigmoid(g)
            act[GATE, r, cut] = (h * u * s * (1.0 + g * (1.0 - s))).astype(BF16)
            act[UP, r, cut] = (h * g * s).astype(BF16)
            return 0

        lax.fori_loop(0, rows // tile, body, 0)

    def share(m, c):
        return go.send(act.at[m, top, cuts[c]], act.at[m, low, cuts[c]], beside[m])

    ends = []
    back_out = xs

    def grads(m, t, c):
        cut, q, other = cuts[c], spot[m], 1 - spot[m]

        def term(q, s):
            return dot(lhs(t, span(q, s)), act[m, :, cut], first)

        pair_out[m, 0, :, cut] = term(other, 1 - at.core).astype(BF16)
        to_far = go.send(pair_out.at[m, 0, :, cut], pair_in.at[m, 0, :, cut], pair)
        acc[m, pl.ds(0, block), cut] = term(other, at.core)
        pair_out[m, 1, :, cut] = term(q, 1 - at.core).astype(BF16)
        to_pair = go.send(pair_out.at[m, 1, :, cut], pair_in.at[m, 1, :, cut], pair)
        to_far.wait_recv()
        both = acc[m, pl.ds(0, block), cut] + pair_in[m, 0, :, cut].astype(F32)
        pre_out[m, :, cut] = both.astype(BF16)
        to_other = go.send(pre_out.at[m, :, cut], near_in.at[m, :, cut], across[m])
        owns[m][:, cut] = term(q, at.core)
        ends.append((m, c, to_other, to_pair))

    back, back_grad = [], []

    def send_out(half):
        r = low if half else top
        val = dot(act[DOWN, r], full[DOWN], turned)
        back_out[0, half] = val.astype(BF16).reshape(shape + (half_d,))
        back.extend(spread(back_out.at[0], back_in.at[0], at.to_y, half))

    def send_grad(half):
        r = low if half else top
        val = dot(act[GATE, r], full[GATE], turned) + dot(act[UP, r], full[UP], turned)
        back_out[1, half] = val.astype(BF16).reshape(shape + (half_d,))
        back_grad.extend(spread(back_out.at[1], back_in.at[1], at.to_x, half))

    pre, got = {}, {}
    far[UP, 0] = forward(UP, cuts[0], coming[UP, 0])
    wait_in(x_rows)
    for m in (GATE, UP):
        begin(m, 0, 0)
    for m in (GATE, UP):
        pre[m, 0] = finish(m, 0, 0, far[m, 0])
    for c in range(2):
        far[DOWN, c] = forward(DOWN, cuts[c], coming[DOWN, c])
    for m in (GATE, UP):
        begin(m, 0, 1)
    far[GATE, 1] = forward(GATE, cuts[1], coming[GATE, 1])
    wait_in(og_rows)
    for c in range(2):
        begin(DOWN, 1, c)
        pre[DOWN, c] = finish(DOWN, 1, c, far[DOWN, c])
    pre[GATE, 0].wait_recv()
    pre[UP, 0].wait_recv()
    make_hidden(0)
    got[DOWN, 0] = share(DOWN, 0)
    pre[GATE, 1] = finish(GATE, 0, 1, far[GATE, 1])
    far[UP, 1] = forward(UP, cuts[1], coming[UP, 1])
    pre[UP, 1] = finish(UP, 0, 1, far[UP, 1])
    pre[DOWN, 0].wait_recv()
    make_grads(0)
    for m in (GATE, UP):
        got[m, 0] = share(m, 0)
    pre[GATE, 1].wait_recv()
    pre[UP, 1].wait_recv()
    make_hidden(1)
    got[DOWN, 1] = share(DOWN, 1)
    weights = list(coming.values()) + list(far.values()) + [pair_of[0] for pair_of in nearby.values()]
    go.drain(x_rows + og_rows + weights)
    send_out(0)
    pre[DOWN, 1].wait_recv()
    make_grads(1)
    for m in (GATE, UP):
        got[m, 1] = share(m, 1)
    send_grad(0)

    go.drain(list(pre.values()))
    got[GATE, 0].wait_recv()
    grads(GATE, 0, 0)
    got[DOWN, 0].wait_recv()
    got[DOWN, 1].wait_recv()
    send_out(1)
    got[UP, 0].wait_recv()
    grads(UP, 0, 0)
    grads(DOWN, 1, 0)
    got[GATE, 1].wait_recv()
    got[UP, 1].wait_recv()
    send_grad(1)
    grads(GATE, 0, 1)
    grads(UP, 0, 1)
    grads(DOWN, 1, 1)

    wait_in(back)
    met = None
    for half in range(2):
        slot = back_in[0, half].reshape(rows, half_d)
        output[:, y_cols(half)] = dot(weighted[...], slot, first).astype(BF16)
        val = dot(slot, cotangent[:, y_cols(half)], turned)
        met = val if met is None else met + val
    met = jnp.where(pick[...].astype(F32) > 0.0, met, 0.0)
    for k in range(ids.shape[0]):
        hit = jnp.where(ids[pl.ds(k, 1), :] == target, met, 0.0)
        grad_gates[pl.ds(k, 1), :] = jnp.sum(hit, axis=0, keepdims=True)
    wait_in(back_grad)
    for half in range(2):
        for k in range(2):
            slot = back_in[1, half, :, :, pl.ds(2 * k * block, 2 * block)].reshape(rows, 2 * block)
            grad_tokens[:, x_cols(half, k)] = dot(pick[...], slot, first).astype(BF16)
    for m, c, to_other, to_pair in ends:
        cut = cuts[c]
        to_pair.wait_recv()
        to_other.wait_recv()
        owns[m][:, cut] += pair_in[m, 1, :, cut].astype(F32) + near_in[m, :, cut].astype(F32)
    go.drain(go.pending)
    assert (go.sending, go.remote, go.near) == (SENDS, REMOTE, LOCAL)


def stay(x):
    return pltpu.with_memory_space_constraint(x, pltpu.MemorySpace.HBM)


def layer_call(groups, ws, ids, gates, tokens, cotangent):
    dma = pltpu.SemaphoreType.DMA
    block, ff = ws[0].shape
    tok, width = tokens.shape
    rows = groups * MOST
    wide = (2, 2, groups, MOST, width // 2)
    vmem = pltpu.VMEM
    return pl.pallas_call(
        functools.partial(layer_kernel, groups),
        out_shape=[jax.ShapeDtypeStruct((block, ff), F32)] * 3
        + [jax.ShapeDtypeStruct((tok, width), BF16)] * 2
        + [jax.ShapeDtypeStruct(ids.shape, F32)],
        in_specs=[HBM] * 7,
        out_specs=[VMEM] * 6,
        scratch_shapes=[
            vmem((3, 4 * block, ff), BF16),
            vmem(wide, BF16),
            vmem(wide, BF16),
            vmem((3, 2 * rows, ff), F32),
            vmem((3, block, ff), BF16),
            vmem((3, rows, ff), BF16),
            vmem((3, 2 * rows, ff), BF16),
            vmem((3, 2, block, ff), BF16),
            vmem((3, 2, block, ff), BF16),
            vmem((3, block, ff), BF16),
            vmem(wide, BF16),
            vmem(ids.shape, ids.dtype),
            vmem(gates.shape, gates.dtype),
            vmem((tok, width), BF16),
            vmem((tok, width), BF16),
            vmem((rows, tok), BF16),
            vmem((rows, tok), BF16),
            dma((SENDS,)),
            dma((REMOTE,)),
            dma((LOCAL,)),
            pltpu.SemaphoreType.REGULAR,
            pltpu.SemaphoreType.REGULAR,
        ],
        compiler_params=pltpu.CompilerParams(
            collective_id=0, has_side_effects=True, vmem_limit_bytes=41 * 2**20
        ),
    )(*map(stay, [*ws, ids, gates, tokens, cotangent]))


def store_kernel(*refs):
    n = len(refs) // 2
    srcs, dsts, sems = refs[:n], refs[n : 2 * n], refs[2 * n]
    copies = [pltpu.make_async_copy(srcs[i], dsts[i], sems.at[i]) for i in range(n)]
    for copy in copies:
        copy.start()
    for copy in copies:
        copy.wait()


def store_call(arrays):
    return pl.pallas_call(
        store_kernel,
        out_shape=[jax.ShapeDtypeStruct(a.shape, a.dtype) for a in arrays],
        in_specs=[VMEM] * len(arrays),
        out_specs=[HBM] * len(arrays),
        scratch_shapes=[pltpu.SemaphoreType.DMA((len(arrays),))],
        compiler_params=pltpu.CompilerParams(vmem_limit_bytes=2**20),
    )(*arrays)


def routes(expert_ids, gate_vals, groups):
    per_index = EXPERTS // groups
    window = WAVE * groups
    tok_count = expert_ids.shape[0]
    local_index = expert_ids % per_index
    window_slot = jnp.where(
        local_index < WAVE, expert_ids // per_index * WAVE + local_index, window
    )
    slot_is = window_slot[:, :, None] == jnp.arange(window, dtype=jnp.int32)[None, None, :]
    chosen = jnp.any(slot_is, axis=1)
    gate_of = jnp.sum(jnp.where(slot_is, gate_vals.astype(F32)[:, :, None], 0.0), axis=1)
    tok = jnp.arange(tok_count, dtype=jnp.int32)
    before = (tok[:, None] > tok[None, :]).astype(BF16)
    rank = dot(before, chosen.astype(BF16), ((1,), (0,))).astype(jnp.int32)
    place = chosen[:, :, None] & (
        rank[:, :, None] == jnp.arange(MOST, dtype=jnp.int32)[None, None, :]
    )
    pick = place.astype(BF16).reshape(tok_count, window * MOST)
    weighted = (
        jnp.where(place, gate_of[:, :, None], 0.0).astype(BF16).reshape(tok_count, window * MOST)
    )
    return slot_is, place, pick, weighted


def on_device(tokens, expert_ids, gate_vals, w_gate, w_up, w_down, cotangent):
    groups = lax.axis_size("expert")
    columns = lax.axis_size("fsdp")
    side = lax.axis_index("fsdp") % 2
    tok_count, width = tokens.shape
    block = w_gate.shape[1]
    rows = groups * MOST
    sides = [[i for i in range(columns) if i % 2 == s] for s in (0, 1)]
    pairs = [(i, i ^ 1) for i in range(columns)]

    def swap(x):
        return lax.ppermute(x, "fsdp", pairs)

    def gather(w):
        return lax.all_gather(w[0], "fsdp", axis_index_groups=sides, axis=0, tiled=True)

    def scatter(x):
        return lax.psum_scatter(
            x.astype(BF16), "fsdp", scatter_dimension=0, axis_index_groups=sides, tiled=True
        ).astype(F32)[None]

    def cut(x, odd):
        return jnp.concatenate(
            [x[:, (2 * k + odd) * block : (2 * k + odd + 1) * block] for k in range(columns // 2)],
            axis=1,
        )

    def halves(x):
        even, odd = cut(x, 0), cut(x, 1)
        return jnp.where(side == 0, even, odd), jnp.where(side == 0, odd, even)

    def whole_rows(mine, other):
        even, odd = jnp.where(side == 0, mine, other), jnp.where(side == 0, other, mine)
        parts = []
        for k in range(columns // 2):
            here = slice(k * block, (k + 1) * block)
            parts += [even[:, here], odd[:, here]]
        return jnp.concatenate(parts, axis=1)

    def exchange(mine, other):
        packed = jnp.stack(
            [mine.reshape(groups, MOST, width // 2), other.reshape(groups, MOST, width // 2)],
            axis=1,
        )
        there = lax.all_to_all(packed, "expert", split_axis=0, concat_axis=0, tiled=True)
        return there[:, 0].reshape(rows, width // 2), there[:, 1].reshape(rows, width // 2)

    square = columns == 8 and groups == 4
    first = ((0,), (0,))
    if square:
        results = layer_call(
            groups, [w_gate[0], w_up[0], w_down[0]], expert_ids.T, gate_vals.T, tokens, cotangent
        )
        *grad_w, output, grad_tokens, grad_gates = store_call(results)
        return (output, grad_tokens, grad_gates.T, *(g[None] for g in grad_w))
    slot_is, place, pick, weighted = routes(expert_ids, gate_vals, groups)
    full_gate, full_up, full_down = gather(w_gate), gather(w_up), gather(w_down)
    row_mine, row_other = exchange(*halves(dot(pick, tokens, first).astype(BF16)))
    og_mine, og_other = exchange(*halves(dot(weighted, cotangent, first).astype(BF16)))
    row_in = jnp.concatenate([row_mine, swap(row_other)], axis=0)
    out_grad = jnp.concatenate([og_mine, swap(og_other)], axis=0)

    def summed(x):
        return x[:rows] + swap(x[rows:].astype(BF16)).astype(F32)

    def both(x):
        return jnp.concatenate([x, swap(x)], axis=0)

    plain, turned = ((1,), (0,)), ((1,), (1,))
    gate_pre = summed(dot(row_in, full_gate, plain))
    up_pre = summed(dot(row_in, full_up, plain))
    sigmoid_g = jax.nn.sigmoid(gate_pre)
    hidden = (gate_pre * sigmoid_g * up_pre).astype(BF16)
    hidden_grad = summed(dot(out_grad, full_down, plain))
    gate_grad = (
        hidden_grad * up_pre * sigmoid_g * (1.0 + gate_pre * (1.0 - sigmoid_g))
    ).astype(BF16)
    up_grad = (hidden_grad * gate_pre * sigmoid_g).astype(BF16)
    hidden, gate_grad, up_grad = both(hidden), both(gate_grad), both(up_grad)
    grad_w_down = scatter(dot(out_grad, hidden, first))
    grad_w_gate = scatter(dot(row_in, gate_grad, first))
    grad_w_up = scatter(dot(row_in, up_grad, first))
    expert_out = dot(hidden, full_down, turned).astype(BF16)
    slot_grad = (dot(gate_grad, full_gate, turned) + dot(up_grad, full_up, turned)).astype(BF16)
    outs = exchange(expert_out[:rows], swap(expert_out[rows:]))
    grads = exchange(slot_grad[:rows], swap(slot_grad[rows:]))

    slot_out = whole_rows(*outs)
    output = dot(weighted, slot_out, plain).astype(BF16)
    grad_tokens = dot(pick, whole_rows(*grads), plain).astype(BF16)
    met = dot(cotangent, slot_out, turned)
    met = jnp.sum(jnp.where(place, met.reshape(place.shape), 0.0), axis=2)
    grad_gates = jnp.sum(jnp.where(slot_is, met[:, None, :], 0.0), axis=2)
    return (output, grad_tokens, grad_gates, grad_w_gate, grad_w_up, grad_w_down)


def solution(mesh):
    token = P(("expert", "fsdp"), None)
    weight = P("expert", "fsdp", None)
    return jax.shard_map(
        on_device,
        mesh=mesh,
        in_specs=(token, token, token, weight, weight, weight, token),
        out_specs=(token, token, token, weight, weight, weight),
        check_vma=False,
    )
```
